32 devices in a mesh: ew: 8 (over y, x, core), ns: 4 (over z).
Axes of the slice: x: 2, y: 2, z: 4, core: 2. Of those that a mesh axis runs over, the one named last changes fastest.
Arguments:
- fluid: float32 [19, 32, 64, 1024], P(None, None, 'ew', 'ns'), may hold values from 0 to 0.6, as said below
- heat: float32 [7, 32, 64, 1024], P(None, None, 'ew', 'ns'), may hold values from 0 to 0.4, as said below
- solid_mask: int32 [32, 64, 1024], P(None, 'ew', 'ns'), may hold values 0 or 1
- inflow_type: int32 [32, 1024], P(None, 'ns'), may hold values from 0 to 2
Outputs:
- fluid_next: float32 [19, 32, 64, 1024], P(None, None, 'ew', 'ns')
- heat_next: float32 [7, 32, 64, 1024], P(None, None, 'ew', 'ns')
The draws below stay inside these ranges and needn't reach their ends.
Inputs may be any that keep to these rules, and one draw needn't show every extreme that they name: `fluid`: each population is positive. `heat`: each population is positive.
All inputs are finite; a program needn't handle non-finite values. No bound on the sum of `solid_mask` on one device may be relied on, other than what follows from the above.
Results may differ from the reference program's by a relative error of at most 0.0001.
Values sent between devices are 32-bit elements; how exact they have to be, the bound alone decides.
No kernel may reach another device: no remote copies, remote signals or barrier semaphores. Data moves between devices by JAX's collectives and lax.ppermute only.
A program may use at most 192 MiB of HBM per device.

```python
import jax
import jax.numpy as jnp

CZ = 32
STEPS = 2
NX = 64
NY = 1024


def draw_fluid(key, part):
    weights = jnp.array([1.0 / 3.0] + [1.0 / 18.0] * 6 + [1.0 / 36.0] * 12, jnp.float32)[:, None, None, None]
    noise = jax.random.uniform(key, (19, CZ, NX, NY), jnp.float32, -1.0, 1.0)
    return weights * (1.0 + 0.5 * noise)


def draw_heat(key, part):
    weights = jnp.array([0.25] + [0.125] * 6, jnp.float32)[:, None, None, None]
    noise = jax.random.uniform(key, (7, CZ, NX, NY), jnp.float32, -1.0, 1.0)
    return weights * (1.0 + 0.5 * noise)


def place_ends(entries, own_key, low, top_value):
    longest = entries.shape.index(max(entries.shape))
    spots = []
    for shift in (0, 1):
        where = [jax.random.randint(jax.random.fold_in(own_key, axis), (), 0, length) for axis, length in enumerate(entries.shape)]
        where[longest] = (where[longest] + shift) % entries.shape[longest]
        spots.append(tuple(where))
    return entries.at[spots[0]].set(low).at[spots[1]].set(top_value)


def setup_inputs(seed: int = 0) -> dict:
    key_list = jax.random.split(jax.random.key(seed), 5)
    return {
        "fluid": draw_fluid(jax.random.fold_in(key_list[4], 71), 0),
        "heat": draw_heat(jax.random.fold_in(key_list[4], 71), 0),
        "solid_mask": place_ends((jax.random.randint(key_list[2], (CZ, NX, NY), 0, 8) < 1).astype(jnp.int32), jax.random.fold_in(key_list[2], 1), 0, 1),
        "inflow_type": place_ends(jax.random.randint(key_list[3], (CZ, NY), 0, 3), jax.random.fold_in(key_list[3], 1), 0, 2).astype(jnp.int32),
    }


FLUID_DIRS = [(0, 0, 0), (1, 0, 0), (-1, 0, 0), (0, 1, 0), (0, -1, 0), (0, 0, 1), (0, 0, -1), (1, 1, 0), (-1, -1, 0), (1, -1, 0), (-1, 1, 0), (1, 0, 1), (-1, 0, -1), (1, 0, -1), (-1, 0, 1), (0, 1, 1), (0, -1, -1), (0, 1, -1), (0, -1, 1)]
FLUID_WEIGHTS = [1.0 / 3.0] + [1.0 / 18.0] * 6 + [1.0 / 36.0] * 12
THERMAL_SHARES = [0.25] + [0.125] * 6
FLOW_COLLIDE_TAU = 0.6
TAU_HEAT = 0.8
FLOAT_COUPLING = 0.02
INFLOW_SPEED = 0.08
COOLING = 0.2
SURROUNDING_WARM = 1.0


def direction(stencil_number):
    return FLUID_DIRS[stencil_number if stencil_number < 19 else stencil_number - 19]


def opposite(stencil_number):
    base = stencil_number if stencil_number < 19 else stencil_number - 19
    cx, cy, cz = FLUID_DIRS[base]
    found = FLUID_DIRS.index((-cx, -cy, -cz))
    return found if stencil_number < 19 else found + 19


def rested_populace(stencil_number, matter_amount, speed_xaxis, speed_yaxis, speed_zaxis, cell_warmth):
    cx, cy, cz = direction(stencil_number)
    projected_speed = cx * speed_xaxis + cy * speed_yaxis + cz * speed_zaxis
    if stencil_number < 19:
        speed_sq = speed_xaxis * speed_xaxis + speed_yaxis * speed_yaxis + speed_zaxis * speed_zaxis
        return FLUID_WEIGHTS[stencil_number] * matter_amount * (1.0 + 3.0 * projected_speed + 4.5 * projected_speed * projected_speed - 1.5 * speed_sq)
    return THERMAL_SHARES[stencil_number - 19] * cell_warmth * (1.0 + 4.0 * projected_speed)


def collide(particle_tables):
    matter_amount = jnp.sum(particle_tables[:19], axis=0)
    mom_x = sum(FLUID_DIRS[i][0] * particle_tables[i] for i in range(1, 19) if FLUID_DIRS[i][0] != 0)
    mom_y = sum(FLUID_DIRS[i][1] * particle_tables[i] for i in range(1, 19) if FLUID_DIRS[i][1] != 0)
    mom_z = sum(FLUID_DIRS[i][2] * particle_tables[i] for i in range(1, 19) if FLUID_DIRS[i][2] != 0)
    speed_xaxis, speed_yaxis, speed_zaxis = mom_x / matter_amount, mom_y / matter_amount, mom_z / matter_amount
    cell_warmth = jnp.sum(particle_tables[19:], axis=0)
    gravity_push = FLOW_COLLIDE_TAU * FLOAT_COUPLING * (cell_warmth - SURROUNDING_WARM)
    result = []
    for stencil_number in range(26):
        if stencil_number < 19:
            receiving_point = rested_populace(stencil_number, matter_amount, speed_xaxis, speed_yaxis, speed_zaxis + gravity_push, cell_warmth)
            result.append(particle_tables[stencil_number] - (particle_tables[stencil_number] - receiving_point) / FLOW_COLLIDE_TAU)
        else:
            receiving_point = rested_populace(stencil_number, matter_amount, speed_xaxis, speed_yaxis, speed_zaxis, cell_warmth)
            result.append(particle_tables[stencil_number] - (particle_tables[stencil_number] - receiving_point) / TAU_HEAT)
    return jnp.stack(result)


def stream(padded, post, particle_tables, solid_pad, solid, kind_pad, outside):
    depth, width, length = particle_tables.shape[1], particle_tables.shape[2], particle_tables.shape[3]
    ghost_vel = INFLOW_SPEED * 0.5 * kind_pad
    ghost_temp = SURROUNDING_WARM - COOLING * kind_pad
    result = []
    for stencil_number in range(26):
        cx, cy, cz = direction(stencil_number)
        ghost = rested_populace(stencil_number, 1.0, ghost_vel, 0.0, 0.0, ghost_temp)
        layer = jnp.where(outside, ghost, padded[stencil_number])
        source = layer[1 - cz:1 - cz + depth, 1 - cx:1 - cx + width, 1 - cy:1 - cy + length]
        blocked = solid_pad[1 - cz:1 - cz + depth, 1 - cx:1 - cx + width, 1 - cy:1 - cy + length] > 0.5
        value = jnp.where(blocked, post[opposite(stencil_number)], source)
        result.append(jnp.where(solid, particle_tables[stencil_number], value))
    return jnp.stack(result)


def reference(fluid, heat, solid_mask, inflow_type):
    particle_tables = jnp.concatenate([fluid, heat], axis=0)
    depth, width, length = solid_mask.shape
    z_index = jnp.arange(depth + 2)[:, None, None]
    x_index = jnp.arange(width + 2)[None, :, None]
    y_index = jnp.arange(length + 2)[None, None, :]
    solid_pad = jnp.pad(solid_mask.astype(jnp.float32), 1)
    solid_pad = jnp.where(z_index == 0, jnp.ones_like(solid_pad), solid_pad)
    type_pad = jnp.pad(inflow_type.astype(jnp.float32), 1)
    kind_pad = jnp.where(x_index == 0, type_pad[:, None, :], jnp.zeros_like(type_pad[:, None, :]))
    outside = (z_index == depth + 1) | (x_index == 0) | (x_index == width + 1) | (y_index == 0) | (y_index == length + 1)
    solid = solid_mask > 0
    for step in range(STEPS):
        post = collide(particle_tables)
        padded = jnp.pad(post, ((0, 0), (1, 1), (1, 1), (1, 1)))
        particle_tables = stream(padded, post, particle_tables, solid_pad, solid, kind_pad, outside)
    return particle_tables[:19], particle_tables[19:]
```

```python
import functools
import math

import jax
import jax.numpy as jnp
from jax import lax
from jax.experimental import pallas as pl
from jax.experimental.pallas import tpu as pltpu
from jax.sharding import PartitionSpec as P

FLUID_DIRS = [
    (0, 0, 0),
    (1, 0, 0),
    (-1, 0, 0),
    (0, 1, 0),
    (0, -1, 0),
    (0, 0, 1),
    (0, 0, -1),
    (1, 1, 0),
    (-1, -1, 0),
    (1, -1, 0),
    (-1, 1, 0),
    (1, 0, 1),
    (-1, 0, -1),
    (1, 0, -1),
    (-1, 0, 1),
    (0, 1, 1),
    (0, -1, -1),
    (0, 1, -1),
    (0, -1, 1),
]
DIRS = FLUID_DIRS + FLUID_DIRS[:7]
NF, NH = 19, 7
NP = NF + NH
OPP = [
    (FLUID_DIRS.index((-c[0], -c[1], -c[2])) + (0 if i < NF else NF)) for i, c in enumerate(DIRS)
]
WEIGHTS = (
    [1.0 / 3.0] + [1.0 / 18.0] * 6 + [1.0 / 36.0] * 12 + [0.25] + [0.125] * 6
)
PLUS = [i for i, c in enumerate(DIRS) if c[0] == 1]
MINUS = [i for i, c in enumerate(DIRS) if c[0] == -1]
TAU = 0.6
TAU_HEAT = 0.8
COUPLING = 0.02
INFLOW_SPEED = 0.08
COOLING = 0.2
MARK = -3.0e38
MASK, KIND = NP, NP + 1
SLOTS = NP + 2
NFACE = NP + 1 + len(PLUS) + 1
TILE = 128
GROUP = 4
GROUPS = SLOTS // GROUP
PITCH = TILE // GROUP


def collided(f):
    pairs = {k: (f[k] + f[k + 1], f[k] - f[k + 1]) for k in range(1, NF, 2)}
    s = {k: v[0] for k, v in pairs.items()}
    d = {k: v[1] for k, v in pairs.items()}
    rho = (f[0] + (s[1] + s[3])) + ((s[5] + s[7]) + (s[9] + s[11])) + ((s[13] + s[15]) + s[17])
    mx = (d[1] + d[7]) + (d[9] + (d[11] + d[13]))
    my = (d[3] + d[7]) + ((d[15] - d[9]) + d[17])
    mz = (d[5] + d[11]) + ((d[15] - d[13]) - d[17])
    g = f[NF:]
    hp = [(g[k] + g[k + 1]) for k in (1, 3, 5)]
    warm = (g[0] + hp[0]) + (hp[1] + hp[2])
    inv = 1.0 / rho
    ux, uy, uz = mx * inv, my * inv, mz * inv
    lifted = uz + TAU * COUPLING * (warm - 1.0)
    root = math.sqrt(4.5)
    ax, ay, az = ux * root, uy * root, lifted * root
    base = 1.0 - (ax * ax + ay * ay + az * az) * (1.0 / 3.0)
    keep = 1.0 - 1.0 / TAU
    r = rho * (1.0 / TAU)
    r18, r36 = r * (1.0 / 18.0), r * (1.0 / 36.0)
    o18, o36 = r18 * (3.0 / root), r36 * (3.0 / root)
    out = [None] * NP
    out[0] = keep * f[0] + (r * (1.0 / 3.0)) * base
    along = {
        1: ax,
        3: ay,
        5: az,
        7: ax + ay,
        9: ax - ay,
        11: ax + az,
        13: ax - az,
        15: ay + az,
        17: ay - az,
    }
    for k, e in along.items():
        w, o = (r18, o18) if k < 7 else (r36, o36)
        even = w * (base + e * e)
        odd = o * e
        out[k] = keep * f[k] + (even + odd)
        out[k + 1] = keep * f[k + 1] + (even - odd)
    hkeep = 1.0 - 1.0 / TAU_HEAT
    t8 = warm * (0.125 / TAU_HEAT)
    out[NF] = hkeep * g[0] + warm * (0.25 / TAU_HEAT)
    t2 = t8 * 4.0
    for k, u in ((1, ux), (3, uy), (5, uz)):
        odd = t2 * u
        out[NF + k] = hkeep * g[k] + (t8 + odd)
        out[NF + k + 1] = hkeep * g[k + 1] + (t8 - odd)
    return out


def ghost(i, kind):
    u = (INFLOW_SPEED * 0.5) * kind
    cx = DIRS[i][0]
    if i < NF:
        return WEIGHTS[i] * (1.0 + 3.0 * cx * u + (4.5 * cx * cx - 1.5) * (u * u))
    return WEIGHTS[i] * (1.0 - COOLING * kind) * (1.0 + 4.0 * cx * u)


def collide_kernel(tiles, *refs):
    fluid, heat, mask = refs[:tiles], refs[tiles : 2 * tiles], refs[2 * tiles : 3 * tiles]
    kind, post, west, east, packed = refs[3 * tiles :]
    width, rows, length = post.shape[0], post.shape[2], post.shape[3]
    lanes = lax.broadcasted_iota(jnp.int32, (rows, TILE), 1)

    def column(x, carry):
        cells = pl.ds(x, rows, stride=width)
        for t in range(tiles):
            span = pl.ds(t * TILE, TILE)
            f = [fluid[t][i, cells] for i in range(NF)]
            f += [heat[t][i, cells] for i in range(NH)]
            solid = mask[t][cells] > 0
            for i, v in enumerate(collided(f)):
                post[x, i, :, span] = jnp.where(solid, MARK, v)
        return carry

    lax.fori_loop(0, width, column, 0)

    def clean(v):
        return jnp.where(v == MARK, 0.0, v)

    for face, near, far, moving in ((west, 0, 1, MINUS), (east, width - 1, width - 2, PLUS)):
        for i in range(NP):
            face[i] = clean(post[near, i])
        face[NP] = jnp.where(post[near, 0] == MARK, 1.0, 0.0)
        for n, i in enumerate(moving):
            face[NP + 1 + n] = clean(post[far, i])
        face[NFACE - 1] = jnp.where(post[far, 0] == MARK, 1.0, 0.0)

    first, last = pl.ds(0, TILE), pl.ds(length - TILE, TILE)
    for group in range(GROUPS):
        total = jnp.zeros((rows, TILE), jnp.float32)
        for x in range(width):
            for k in range(GROUP):
                p = group * GROUP + k
                if p < NP:
                    a, b = post[x, p, :, first], post[x, p, :, last]
                elif p == MASK:
                    cells = pl.ds(x, rows, stride=width)
                    a, b = mask[0][cells], mask[-1][cells]
                    a, b = a.astype(jnp.float32), b.astype(jnp.float32)
                else:
                    a, b = kind[:, first].astype(jnp.float32), kind[:, last].astype(jnp.float32)
                start = k * PITCH + x * 4
                both = pltpu.roll(jnp.where(lanes >= TILE - 2, b, a), (start + 2) % TILE, 1)
                total = jnp.where((lanes >= start) & (lanes < start + 4), both, total)
        packed[group] = clean(total)


def collide_call(fluid, heat, mask, kind):
    depth, width, length = mask.shape
    rows = 8
    block = rows * width
    f32 = jnp.float32
    tiles = length // TILE
    span = range(tiles)
    return pl.pallas_call(
        functools.partial(collide_kernel, tiles),
        grid=(depth // rows,),
        in_specs=[pl.BlockSpec((NF, block, TILE), lambda z, t=t: (0, z, t)) for t in span]
        + [pl.BlockSpec((NH, block, TILE), lambda z, t=t: (0, z, t)) for t in span]
        + [pl.BlockSpec((block, TILE), lambda z, t=t: (z, t)) for t in span]
        + [pl.BlockSpec((rows, length), lambda z: (z, 0))],
        out_specs=[
            pl.BlockSpec((width, NP, rows, length), lambda z: (0, 0, z, 0)),
            pl.BlockSpec((NFACE, rows, length), lambda z: (0, z, 0)),
            pl.BlockSpec((NFACE, rows, length), lambda z: (0, z, 0)),
            pl.BlockSpec((GROUPS, rows, TILE), lambda z: (0, z, 0)),
        ],
        out_shape=[
            jax.ShapeDtypeStruct((width, NP, depth, length), f32),
            jax.ShapeDtypeStruct((NFACE, depth, length), f32),
            jax.ShapeDtypeStruct((NFACE, depth, length), f32),
            jax.ShapeDtypeStruct((GROUPS, depth, TILE), f32),
        ],
        name="collide",
    )(
        *[fluid.reshape(NF, depth * width, length)] * tiles,
        *[heat.reshape(NH, depth * width, length)] * tiles,
        *[mask.reshape(depth * width, length)] * tiles,
        kind,
    )


def ring(v, axis, shift):
    n = lax.axis_size(axis)
    return lax.ppermute(v, axis, [(i, (i + shift) % n) for i in range(n)])


def stream_kernel(
    place,
    fluid,
    heat,
    post,
    west,
    east,
    own,
    cross,
    ours_w,
    ours_e,
    kind,
    fluid_out,
    heat_out,
    a,
    b,
    strip,
    strip2,
    fresh,
    fout,
    hout,
    load_sem,
    fill_sem,
    out_sem,
):
    width, depth, length = post.shape[0], post.shape[2], post.shape[3]
    at_west, at_east = place[0] == 1, place[1] == 1
    at_low, at_high = place[2] == 1, place[3] == 1
    load = pltpu.make_async_copy(post, a.at[pl.ds(2, width)], load_sem)
    load.start()
    tiles = length // TILE
    fills = []
    for t in range(tiles):
        span = pl.ds(t * TILE, TILE)
        fills.append(pltpu.make_async_copy(fluid.at[:, :, span], fout.at[t], fill_sem.at[0, t]))
        fills.append(pltpu.make_async_copy(heat.at[:, :, span], hout.at[t], fill_sem.at[1, t]))
    for copy in fills:
        copy.start()

    shape = (depth, TILE)
    lanes = lax.broadcasted_iota(jnp.int32, shape, 1)
    levels = lax.broadcasted_iota(jnp.int32, shape, 0)
    side, slot, j = lanes // 64, (lanes % 64) // 4, lanes % 4
    ground, top = levels == 0, levels == depth - 1
    lane0, lane127 = lanes == 0, lanes == TILE - 1

    inner = (slot >= 4) & (slot < 4 + width)
    left = slot < 4
    for group in range(GROUPS):
        o, c = own[group], cross[group]
        ow, cw = ours_w[group], ours_w[GROUPS + group]
        oe, ce = ours_e[group], ours_e[GROUPS + group]
        low, high = jnp.where(j < 2, c, o), jnp.where(j < 2, o, c)
        low_w, high_w = jnp.where(j < 2, cw, ow), jnp.where(j < 2, ow, cw)
        low_e, high_e = jnp.where(j < 2, ce, oe), jnp.where(j < 2, oe, ce)
        for k in range(GROUP):
            r = k * PITCH

            def put(lo, hi, shift):
                lo = pltpu.roll(lo, (shift - r) % TILE, 1)
                hi = pltpu.roll(hi, (64 + shift - r) % TILE, 1)
                return jnp.where(side == 0, lo, hi)

            v = jnp.where(
                inner,
                put(low, high, 16),
                jnp.where(
                    left,
                    put(low_w, high_w, 16 - 4 * width),
                    put(low_e, high_e, 16 + 4 * width),
                ),
            )
            strip[group * GROUP + k] = v
    beyond_low = at_low & (side == 0) & (j < 2)
    beyond_high = at_high & (side == 1) & (j >= 2)
    beyond_y = beyond_low | beyond_high
    beyond = beyond_y | (at_west & left) | (at_east & (slot >= 4 + width))
    strip_kind = jnp.where(
        at_west & (slot == 3) & jnp.logical_not(beyond_y),
        pltpu.roll(strip[KIND], TILE - 4, 1),
        0.0,
    )
    strip_solid = strip[MASK] > 0.5
    for i in range(NP):
        v = jnp.where(strip_solid, MARK, strip[i])
        strip[i] = jnp.where(beyond, ghost(i, strip_kind), v)

    kinds = kind[...].astype(jnp.float32)
    for face, edge, near, far, moving in (
        (west, at_west, 1, 0, PLUS),
        (east, at_east, width + 2, width + 3, MINUS),
    ):
        solid = face[NP] > 0.5
        for i in range(NP):
            v = jnp.where(solid, MARK, face[i])
            if i in moving:
                v = jnp.where(edge, ghost(i, kinds) if near == 1 else WEIGHTS[i], v)
            a[near, i] = v
        solid = face[NFACE - 1] > 0.5
        for n, i in enumerate(moving):
            a[far, i] = jnp.where(solid, MARK, face[NP + 1 + n])

    def lifted(v, i):
        cz = DIRS[i][2]
        if cz == 1:
            return jnp.where(ground, MARK, pltpu.roll(v, 1, 0))
        if cz == -1:
            return jnp.where(top, WEIGHTS[i], pltpu.roll(v, depth - 1, 0))
        return v

    def pulled(cells, cols, x, i):
        cx, cy, _ = DIRS[i]
        source = cells(x - cx, i)
        if cy:
            turned = [pltpu.roll(v, cy % TILE, 1) for v in source]
            at = (x - cx + 4) * 4
            if cy == 1:
                col = pltpu.roll(cols[i], lax.rem(2 * TILE - (at + 1), TILE), 1)
                before = [col] + turned[:-1]
                source = [jnp.where(lane0, p, v) for p, v in zip(before, turned)]
            else:
                col = pltpu.roll(cols[i], lax.rem(2 * TILE - 1 - (64 + at + 2), TILE), 1)
                after = turned[1:] + [col]
                source = [jnp.where(lane127, n, v) for n, v in zip(after, turned)]
        return [lifted(v, i) for v in source]

    def pieces(ref, index, i):
        return [ref[index, i, :, pl.ds(t * TILE, TILE)] for t in range(tiles)]

    for i in range(NP):
        cx, cy, _ = DIRS[i]
        v = strip[i]
        if cx or cy:
            v = pltpu.roll(v, (4 * cx + cy) % TILE, 1)
        v = lifted(v, i)
        fresh[i, :, pl.ds(0, TILE)] = jnp.where(v == MARK, strip[OPP[i]], v)
    for z in range(0, depth, 8):
        part = pl.ds(z, 8)
        f = [fresh[i, part, pl.ds(0, TILE)] for i in range(NP)]
        solid = strip[0, part] == MARK
        out_here = beyond[z : z + 8]
        for i, v in enumerate(collided(f)):
            v = jnp.where(solid, MARK, v)
            strip2[i, part] = jnp.where(out_here, ghost(i, strip_kind[z : z + 8]), v)

    load.wait()

    def advance(n, carry):
        x = n - 1
        for i in range(NP):
            vs = pulled(lambda s, p: pieces(a, s + 2, p), strip, x, i)
            backs = pieces(a, x + 2, OPP[i])
            for t, (v, back) in enumerate(zip(vs, backs)):
                fresh[i, :, pl.ds(t * TILE, TILE)] = jnp.where(v == MARK, back, v)
        for z in range(0, depth, 8):
            for t in range(tiles):
                part, span = pl.ds(z, 8), pl.ds(t * TILE, TILE)
                f = [fresh[i, part, span] for i in range(NP)]
                solid = a[x + 2, 0, part, span] == MARK
                for i, v in enumerate(collided(f)):
                    b[n, i, part, span] = jnp.where(solid, MARK, v)
        return carry

    lax.fori_loop(0, width + 2, advance, 0)

    @pl.when(at_west)
    def _():
        for i in PLUS:
            b[0, i] = ghost(i, kinds)

    @pl.when(at_east)
    def _():
        for i in MINUS:
            b[width + 1, i] = jnp.full((depth, length), WEIGHTS[i], jnp.float32)

    for copy in fills:
        copy.wait()
    copies = []
    for i in range(NP):
        buffer, index = (fout, i) if i < NF else (hout, i - NF)
        target = fluid_out if i < NF else heat_out

        def settle(x, carry):
            vs = pulled(lambda s, p: pieces(b, s + 1, p), strip2, x, i)
            backs = pieces(b, x + 1, OPP[i])
            mine = backs if OPP[i] == i else pieces(b, x + 1, i)
            for t, (v, back, me) in enumerate(zip(vs, backs, mine)):
                cells = pl.ds(x, depth, stride=width)
                v = jnp.where(v == MARK, back, v)
                buffer[t, index, cells] = jnp.where(me == MARK, buffer[t, index, cells], v)
            return carry

        lax.fori_loop(0, width, settle, 0)
        for t in range(tiles):
            there = target.at[index, :, pl.ds(t * TILE, TILE)]
            copy = pltpu.make_async_copy(buffer.at[t, index], there, out_sem.at[i, t])
            copy.start()
            copies.append(copy)
    for copy in copies:
        copy.wait()


def stream_call(place, fluid, heat, post, west, east, own, cross, ours_w, ours_e, kind):
    width, _, depth, length = post.shape
    tiles = length // TILE
    f32 = jnp.float32
    vmem = pl.BlockSpec(memory_space=pltpu.VMEM)
    hbm = pl.BlockSpec(memory_space=pl.ANY)
    cells = depth * width
    outs = pl.pallas_call(
        stream_kernel,
        in_specs=[pl.BlockSpec(memory_space=pltpu.SMEM), hbm, hbm, hbm]
        + [vmem, vmem, vmem, vmem, vmem, vmem, vmem],
        out_specs=[hbm, hbm],
        out_shape=[
            jax.ShapeDtypeStruct((NF, cells, length), f32),
            jax.ShapeDtypeStruct((NH, cells, length), f32),
        ],
        scratch_shapes=[
            pltpu.VMEM((width + 4, NP, depth, length), f32),
            pltpu.VMEM((width + 2, NP, depth, length), f32),
            pltpu.VMEM((SLOTS, depth, TILE), f32),
            pltpu.VMEM((NP, depth, TILE), f32),
            pltpu.VMEM((NP, depth, length), f32),
            pltpu.VMEM((tiles, NF, cells, TILE), f32),
            pltpu.VMEM((tiles, NH, cells, TILE), f32),
            pltpu.SemaphoreType.DMA,
            pltpu.SemaphoreType.DMA((2, tiles)),
            pltpu.SemaphoreType.DMA((NP, tiles)),
        ],
        name="stream",
    )(
        place,
        fluid.reshape(NF, cells, length),
        heat.reshape(NH, cells, length),
        post,
        west,
        east,
        own,
        cross,
        ours_w,
        ours_e,
        kind,
    )
    return outs


def per_device(fluid, heat, solid_mask, inflow_type):
    depth, width, length = solid_mask.shape
    post, to_west, to_east, own = collide_call(fluid, heat, solid_mask, inflow_type)
    below = ring(own, "ns", 1)
    above = ring(own, "ns", -1)
    west = ring(to_east, "ew", 1)
    east = ring(to_west, "ew", -1)
    lower = lax.broadcasted_iota(jnp.int32, own.shape, 2) % 4 < 2
    cross = jnp.where(lower, below, above)
    ours = jnp.concatenate([own, cross], axis=0)
    ours_w = ring(ours, "ew", 1)
    ours_e = ring(ours, "ew", -1)
    ew, ns = lax.axis_index("ew"), lax.axis_index("ns")
    place = jnp.stack(
        [ew == 0, ew == lax.axis_size("ew") - 1, ns == 0, ns == lax.axis_size("ns") - 1]
    ).astype(jnp.int32)
    fluid_next, heat_next = stream_call(
        place, fluid, heat, post, west, east, own, cross, ours_w, ours_e, inflow_type
    )
    return (
        fluid_next.reshape(NF, depth, width, length),
        heat_next.reshape(NH, depth, width, length),
    )


def solution(mesh):
    return jax.shard_map(
        per_device,
        mesh=mesh,
        in_specs=(
            P(None, None, "ew", "ns"),
            P(None, None, "ew", "ns"),
            P(None, "ew", "ns"),
            P(None, "ns"),
        ),
        out_specs=(P(None, None, "ew", "ns"), P(None, None, "ew", "ns")),
        check_vma=False,
    )
```

```python
import functools
import math

import jax
import jax.numpy as jnp
from jax import lax
from jax.experimental import pallas as pl
from jax.experimental.pallas import tpu as pltpu
from jax.sharding import PartitionSpec as P

FLUID_DIRS = [
    (0, 0, 0),
    (1, 0, 0),
    (-1, 0, 0),
    (0, 1, 0),
    (0, -1, 0),
    (0, 0, 1),
    (0, 0, -1),
    (1, 1, 0),
    (-1, -1, 0),
    (1, -1, 0),
    (-1, 1, 0),
    (1, 0, 1),
    (-1, 0, -1),
    (1, 0, -1),
    (-1, 0, 1),
    (0, 1, 1),
    (0, -1, -1),
    (0, 1, -1),
    (0, -1, 1),
]
DIRS = FLUID_DIRS + FLUID_DIRS[:7]
NF, NH = 19, 7
NP = NF + NH
OPP = [
    (FLUID_DIRS.index((-c[0], -c[1], -c[2])) + (0 if i < NF else NF)) for i, c in enumerate(DIRS)
]
WEIGHTS = (
    [1.0 / 3.0] + [1.0 / 18.0] * 6 + [1.0 / 36.0] * 12 + [0.25] + [0.125] * 6
)
PLUS = [i for i, c in enumerate(DIRS) if c[0] == 1]
MINUS = [i for i, c in enumerate(DIRS) if c[0] == -1]
TAU = 0.6
TAU_HEAT = 0.8
COUPLING = 0.02
INFLOW_SPEED = 0.08
COOLING = 0.2
MARK = float("nan")
MASK, KIND = NP, NP + 1
SLOTS = NP + 2
NMOVE = len(PLUS)
NFACE = NMOVE + 1
TILE = 128
GROUP = 4
GROUPS = SLOTS // GROUP
PITCH = TILE // GROUP


def collided(f, solid):
    pairs = {k: (f[k] + f[k + 1], f[k] - f[k + 1]) for k in range(1, NF, 2)}
    s = {k: v[0] for k, v in pairs.items()}
    d = {k: v[1] for k, v in pairs.items()}
    rho = (f[0] + (s[1] + s[3])) + ((s[5] + s[7]) + (s[9] + s[11])) + ((s[13] + s[15]) + s[17])
    mx = (d[1] + d[7]) + (d[9] + (d[11] + d[13]))
    my = (d[3] + d[7]) + ((d[15] - d[9]) + d[17])
    mz = (d[5] + d[11]) + ((d[15] - d[13]) - d[17])
    g = f[NF:]
    hp = [(g[k] + g[k + 1]) for k in (1, 3, 5)]
    warm = (g[0] + hp[0]) + (hp[1] + hp[2])
    inv = 1.0 / rho
    ux, uy, uz = mx * inv, my * inv, mz * inv
    lifted = uz + TAU * COUPLING * (warm - 1.0)
    root = math.sqrt(4.5)
    ax, ay, az = ux * root, uy * root, lifted * root
    base = 1.0 - (ax * ax + ay * ay + az * az) * (1.0 / 3.0)
    keep = 1.0 - 1.0 / TAU
    r = jnp.where(solid, MARK, rho * (1.0 / TAU))
    r18, r36 = r * (1.0 / 18.0), r * (1.0 / 36.0)
    o18, o36 = r18 * (3.0 / root), r36 * (3.0 / root)
    out = [None] * NP
    out[0] = keep * f[0] + (r * (1.0 / 3.0)) * base
    along = {
        1: ax,
        3: ay,
        5: az,
        7: ax + ay,
        9: ax - ay,
        11: ax + az,
        13: ax - az,
        15: ay + az,
        17: ay - az,
    }
    for k, e in along.items():
        w, o = (r18, o18) if k < 7 else (r36, o36)
        even = w * (base + e * e)
        odd = o * e
        out[k] = keep * f[k] + (even + odd)
        out[k + 1] = keep * f[k + 1] + (even - odd)
    hkeep = 1.0 - 1.0 / TAU_HEAT
    t8 = jnp.where(solid, MARK, warm * (0.125 / TAU_HEAT))
    out[NF] = hkeep * g[0] + (t8 + t8)
    t2 = t8 * 4.0
    for k, u in ((1, ux), (3, uy), (5, uz)):
        odd = t2 * u
        out[NF + k] = hkeep * g[k] + (t8 + odd)
        out[NF + k + 1] = hkeep * g[k + 1] + (t8 - odd)
    return out


def ghost(i, kind):
    u = (INFLOW_SPEED * 0.5) * kind
    cx = DIRS[i][0]
    if i < NF:
        return WEIGHTS[i] * (1.0 + 3.0 * cx * u + (4.5 * cx * cx - 1.5) * (u * u))
    return WEIGHTS[i] * (1.0 - COOLING * kind) * (1.0 + 4.0 * cx * u)


def marked(v):
    return v != v


def clean(v):
    return jnp.where(marked(v), 0.0, v)


def collide_kernel(tiles, *refs):
    fluid, heat, mask = refs[:tiles], refs[tiles : 2 * tiles], refs[2 * tiles : 3 * tiles]
    post, west, east = refs[3 * tiles :]
    width, rows = post.shape[0], post.shape[2]

    def column(x, carry):
        cells = pl.ds(x, rows, stride=width)
        for t in range(tiles):
            span = pl.ds(t * TILE, TILE)
            f = [fluid[t][i, cells] for i in range(NF)]
            f += [heat[t][i, cells] for i in range(NH)]
            for i, v in enumerate(collided(f, mask[t][cells] > 0)):
                post[x, i, :, span] = v
        return carry

    lax.fori_loop(0, width, column, 0)

    for face, near, moving in ((west, 0, MINUS), (east, width - 1, PLUS)):
        for t in range(tiles):
            span = pl.ds(t * TILE, TILE)
            for n, i in enumerate(moving):
                face[n * tiles + t] = clean(post[near, i, :, span])
            face[NMOVE * tiles + t] = jnp.where(marked(post[near, 0, :, span]), 1.0, 0.0)


def column_kernel(width, *refs):
    fluid, heat, mask, kind, packed = refs[:2], refs[2:4], refs[4:6], refs[6:8], refs[8]
    rows = packed.shape[1]
    lanes = lax.broadcasted_iota(jnp.int32, (rows, TILE), 1)
    start, stop = lanes < 2, lanes >= TILE - 2

    def ends(pair, x):
        a, b = (v.astype(jnp.float32) for v in pair)
        both = jnp.where(stop, b, jnp.where(start, a, 0.0))
        return pltpu.roll(both, (x * 4 + 2) % TILE, 1)

    def gathered(read):
        total = ends(read(0), 0)
        for x in range(1, width):
            total = total + ends(read(x), x)
        return total

    def cells(x):
        return pl.ds(x, rows, stride=width)

    f = [gathered(lambda x: [r[i, cells(x)] for r in fluid]) for i in range(NF)]
    f += [gathered(lambda x: [r[i, cells(x)] for r in heat]) for i in range(NH)]
    solid = gathered(lambda x: [r[cells(x)] for r in mask])
    idle = (solid > 0.5) | (lanes >= 4 * width)
    out = [jnp.where(idle, 0.0, v) for v in collided(f, solid > 0.5)]
    out += [solid, gathered(lambda x: [r[...] for r in kind])]
    for group in range(GROUPS):
        total = out[group * GROUP]
        for k in range(1, GROUP):
            total = total + pltpu.roll(out[group * GROUP + k], k * PITCH, 1)
        packed[group] = total


def column_call(fluid, heat, mask, kind):
    depth, width, length = mask.shape
    rows = 8
    block = rows * width
    ends = (0, length // TILE - 1)
    return pl.pallas_call(
        functools.partial(column_kernel, width),
        grid=(depth // rows,),
        in_specs=[pl.BlockSpec((NF, block, TILE), lambda z, t=t: (0, z, t)) for t in ends]
        + [pl.BlockSpec((NH, block, TILE), lambda z, t=t: (0, z, t)) for t in ends]
        + [pl.BlockSpec((block, TILE), lambda z, t=t: (z, t)) for t in ends]
        + [pl.BlockSpec((rows, TILE), lambda z, t=t: (z, t)) for t in ends],
        out_specs=pl.BlockSpec((GROUPS, rows, TILE), lambda z: (0, z, 0)),
        out_shape=jax.ShapeDtypeStruct((GROUPS, depth, TILE), jnp.float32),
        cost_estimate=cost(depth * width * length, 2),
        compiler_params=pltpu.CompilerParams(vmem_limit_bytes=12 * 2**20),
        name="columns",
    )(
        *[in_hbm(fluid.reshape(NF, depth * width, length))] * 2,
        *[in_hbm(heat.reshape(NH, depth * width, length))] * 2,
        *[in_hbm(mask.reshape(depth * width, length))] * 2,
        *[kind] * 2,
    )


def in_hbm(v):
    return pltpu.with_memory_space_constraint(v, pltpu.HBM)


def cost(cells, passes):
    return pl.CostEstimate(
        flops=300 * cells * passes, bytes_accessed=4 * NP * cells * passes, transcendentals=0
    )


def collide_call(fluid, heat, mask):
    depth, width, length = mask.shape
    rows = 8
    block = rows * width
    f32 = jnp.float32
    tiles = length // TILE
    span = range(tiles)
    return pl.pallas_call(
        functools.partial(collide_kernel, tiles),
        grid=(depth // rows,),
        in_specs=[pl.BlockSpec((NF, block, TILE), lambda z, t=t: (0, z, t)) for t in span]
        + [pl.BlockSpec((NH, block, TILE), lambda z, t=t: (0, z, t)) for t in span]
        + [pl.BlockSpec((block, TILE), lambda z, t=t: (z, t)) for t in span],
        out_specs=[
            pl.BlockSpec((width, NP, rows, length), lambda z: (0, 0, z, 0)),
            pl.BlockSpec((NFACE * tiles, rows, TILE), lambda z: (0, z, 0)),
            pl.BlockSpec((NFACE * tiles, rows, TILE), lambda z: (0, z, 0)),
        ],
        out_shape=[
            jax.ShapeDtypeStruct((width, NP, depth, length), f32),
            jax.ShapeDtypeStruct((NFACE * tiles, depth, TILE), f32),
            jax.ShapeDtypeStruct((NFACE * tiles, depth, TILE), f32),
        ],
        cost_estimate=cost(depth * width * length, 2),
        compiler_params=pltpu.CompilerParams(vmem_limit_bytes=16 * 2**20),
        name="collide",
    )(
        *[in_hbm(fluid.reshape(NF, depth * width, length))] * tiles,
        *[in_hbm(heat.reshape(NH, depth * width, length))] * tiles,
        *[in_hbm(mask.reshape(depth * width, length))] * tiles,
    )


class Lanes:
    def __init__(self, depth, width, place):
        shape = (depth, TILE)
        lane = lax.broadcasted_iota(jnp.int32, shape, 1)
        level = lax.broadcasted_iota(jnp.int32, shape, 0)
        self.side, self.slot, self.j = lane // 64, (lane % 64) // 4, lane % 4
        self.ground, self.top = level == 0, level == depth - 1
        self.first, self.last = lane == 0, lane == TILE - 1
        self.west, self.east = place[0] == 1, place[1] == 1
        low = (place[2] == 1) & (self.side == 0) & (self.j < 2)
        high = (place[3] == 1) & (self.side == 1) & (self.j >= 2)
        self.beyond_y = low | high


def strip_kernel(width, place, own, even, odd, west, east, strip, to_west, to_east):
    depth = own.shape[1]
    at = Lanes(depth, width, place)
    flip = place[4] == 1
    slots_w = [None] * NFACE
    slots_e = [None] * NFACE
    near_j = at.j < 2
    for group in range(GROUPS):
        o = own[group]
        above = jnp.where(flip, odd[group], even[group])
        below = jnp.where(flip, even[group], odd[group])
        low, high = jnp.where(near_j, below, o), jnp.where(near_j, o, above)
        for k in range(GROUP):
            p = group * GROUP + k
            v = jnp.where(
                at.side == 0,
                pltpu.roll(low, (16 - k * PITCH) % TILE, 1),
                pltpu.roll(high, (80 - k * PITCH) % TILE, 1),
            )
            strip[p] = v
            if p in MINUS or p == MASK:
                n = NMOVE if p == MASK else MINUS.index(p)
                slots_w[n] = pltpu.roll(v, (4 * n - 16) % TILE, 1)
            if p in PLUS or p == MASK:
                n = NMOVE if p == MASK else PLUS.index(p)
                slots_e[n] = pltpu.roll(v, (4 * n - 12 - 4 * width) % TILE, 1)
    for out, face, slots in ((to_west, west, slots_w), (to_east, east, slots_e)):
        for n in range(face.shape[0]):
            out[n] = face[n]
        total = jnp.zeros_like(slots[0])
        for n, v in enumerate(slots):
            total = jnp.where(at.slot == n, v, total)
        out[face.shape[0]] = total
    solid = strip[MASK] > 0.5
    for i in range(NP):
        strip[i] = jnp.where(at.beyond_y, WEIGHTS[i], jnp.where(solid, MARK, strip[i]))


def strip_call(width, place, own, even, odd, west, east):
    _, depth, _ = own.shape
    f32 = jnp.float32
    vmem = pl.BlockSpec(memory_space=pltpu.VMEM)
    return pl.pallas_call(
        functools.partial(strip_kernel, width),
        in_specs=[pl.BlockSpec(memory_space=pltpu.SMEM)] + [vmem] * 5,
        out_specs=[vmem, vmem, vmem],
        out_shape=[
            jax.ShapeDtypeStruct((SLOTS, depth, TILE), f32),
            jax.ShapeDtypeStruct((west.shape[0] + 1, depth, TILE), f32),
            jax.ShapeDtypeStruct((west.shape[0] + 1, depth, TILE), f32),
        ],
        compiler_params=pltpu.CompilerParams(vmem_limit_bytes=8 * 2**20),
        name="strips",
    )(place, own, even, odd, west, east)


def raised(v, i, at):
    depth = v.shape[0]
    cz = DIRS[i][2]
    if cz == 1:
        return jnp.where(at.ground, MARK, pltpu.roll(v, 1, 0))
    if cz == -1:
        return jnp.where(at.top, WEIGHTS[i], pltpu.roll(v, depth - 1, 0))
    return v


def pieces(ref, index, i, tiles):
    return [ref[index, i, :, pl.ds(t * TILE, TILE)] for t in range(tiles)]


def pulled(cells, cols, x, i, at):
    cx, cy, _ = DIRS[i]
    source = cells(x - cx, i)
    if cy:
        turned = [pltpu.roll(v, cy % TILE, 1) for v in source]
        lane = (x - cx + 4) * 4
        if cy == 1:
            col = pltpu.roll(cols[i], lax.rem(2 * TILE - (lane + 1), TILE), 1)
            before = [col] + turned[:-1]
            source = [jnp.where(at.first, p, v) for p, v in zip(before, turned)]
        else:
            col = pltpu.roll(cols[i], lax.rem(2 * TILE - 1 - (64 + lane + 2), TILE), 1)
            after = turned[1:] + [col]
            source = [jnp.where(at.last, n, v) for n, v in zip(after, turned)]
    return [raised(v, i, at) for v in source]


def close_strip(strip, kinds, from_west, from_east, solid, at, width):
    kind = jnp.where(at.beyond_y, 0.0, kinds)
    for face, edge, slot, moving in (
        (from_west, at.west, 3, PLUS),
        (from_east, at.east, 4 + width, MINUS),
    ):
        here = at.slot == slot
        for n, i in enumerate(moving):
            v = pltpu.roll(face, (4 * slot - 4 * n) % TILE, 1)
            v = jnp.where(solid, MARK, v)
            v = jnp.where(at.beyond_y, WEIGHTS[i], v)
            v = jnp.where(edge, ghost(i, kind) if slot == 3 else WEIGHTS[i], v)
            strip[i] = jnp.where(here, v, strip[i])


def advance_slab(a, x, near, strip, fresh, out, at):
    depth, length = fresh.shape[1], fresh.shape[2]
    tiles = length // TILE
    for i in range(NP):
        vs = pulled(lambda s, p: pieces(a, s - x + near, p, tiles), strip, x, i, at)
        backs = pieces(a, near, OPP[i], tiles)
        for t, (v, back) in enumerate(zip(vs, backs)):
            fresh[i, :, pl.ds(t * TILE, TILE)] = jnp.where(marked(v), back, v)
    for z in range(0, depth, 8):
        for t in range(tiles):
            part, span = pl.ds(z, 8), pl.ds(t * TILE, TILE)
            f = [fresh[i, part, span] for i in range(NP)]
            solid = marked(a[near, 0, part, span])
            for i, v in enumerate(collided(f, solid)):
                out[i, part, span] = v


def advance_inner_kernel(place, post, strip, next_out, a, fresh, b, load_sem, out_sem):
    width, depth = post.shape[0], post.shape[2]

    def load(x):
        return pltpu.make_async_copy(post.at[x], a.at[x], load_sem.at[x])

    def store(x):
        return pltpu.make_async_copy(b.at[x], next_out.at[x], out_sem.at[x])

    for x in range(width):
        load(x).start()
    at = Lanes(depth, width, place)
    load(0).wait()
    load(1).wait()

    def advance(x, carry):
        load(x + 1).wait()
        advance_slab(a, x, x, strip, fresh, b.at[x], at)
        store(x).start()
        return carry

    lax.fori_loop(1, width - 1, advance, 0)
    for x in range(1, width - 1):
        store(x).wait()


def advance_inner_call(place, post, strip):
    width, _, depth, length = post.shape
    f32 = jnp.float32
    vmem = pl.BlockSpec(memory_space=pltpu.VMEM)
    hbm = pl.BlockSpec(memory_space=pl.ANY)
    return pl.pallas_call(
        advance_inner_kernel,
        in_specs=[pl.BlockSpec(memory_space=pltpu.SMEM), hbm, vmem],
        out_specs=hbm,
        out_shape=jax.ShapeDtypeStruct((width, NP, depth, length), f32),
        scratch_shapes=[
            pltpu.VMEM((width, NP, depth, length), f32),
            pltpu.VMEM((NP, depth, length), f32),
            pltpu.VMEM((width, NP, depth, length), f32),
            pltpu.SemaphoreType.DMA((width,)),
            pltpu.SemaphoreType.DMA((width,)),
        ],
        cost_estimate=cost(depth * width * length, 2),
        compiler_params=pltpu.CompilerParams(vmem_limit_bytes=24 * 2**20),
        name="advance_inner",
    )(place, post, strip)


def ends_of(width):
    return ((0, 1), (1, 2), (width - 2, 3), (width - 1, 4))


def advance_kernel(
    place,
    post,
    west,
    east,
    strip_in,
    kind,
    next_in,
    next_out,
    strip2,
    to_west,
    to_east,
    halo,
    a,
    strip,
    fresh,
    b,
    load_sem,
    out_sem,
):
    width, depth, length = post.shape[0], post.shape[2], post.shape[3]
    tiles = length // TILE
    loads = [
        pltpu.make_async_copy(post.at[x], a.at[n], load_sem.at[n]) for x, n in ends_of(width)
    ]
    for copy in loads:
        copy.start()
    at = Lanes(depth, width, place)
    for p in range(SLOTS):
        strip[p] = strip_in[p]
    ends_w, ends_e = west[NFACE * tiles], east[NFACE * tiles]
    ends = jnp.where(
        at.slot == 3,
        pltpu.roll(ends_w, (12 - 4 * NMOVE) % TILE, 1),
        pltpu.roll(ends_e, (16 + 4 * width - 4 * NMOVE) % TILE, 1),
    )
    kind_end = pltpu.roll(strip[KIND], TILE - 4, 1)
    close_strip(strip, kind_end, ends_w, ends_e, ends > 0.5, at, width)
    halo[0], halo[1] = ends, kind_end
    for n, face in ((2, west), (2 + tiles, east)):
        for t in range(tiles):
            halo[n + t] = face[NMOVE * tiles + t]
    kinds = kind[...].astype(jnp.float32)
    close_faces(a, west, east, halo, kinds, at)

    for i in range(NP):
        cx, cy, _ = DIRS[i]
        v = strip[i]
        if cx or cy:
            v = pltpu.roll(v, (4 * cx + cy) % TILE, 1)
        v = raised(v, i, at)
        fresh[i, :, pl.ds(0, TILE)] = jnp.where(marked(v), strip[OPP[i]], v)
    for z in range(0, depth, 8):
        part = pl.ds(z, 8)
        f = [fresh[i, part, pl.ds(0, TILE)] for i in range(NP)]
        outside = at.beyond_y[z : z + 8]
        for i, v in enumerate(collided(f, marked(strip[0, part]))):
            strip2[i, part] = jnp.where(outside, WEIGHTS[i], v)

    for copy in loads:
        copy.wait()

    def advance(n, carry):
        x = n * (width - 1)
        advance_slab(a, x, 1 + 3 * n, strip, fresh, b.at[n], at)
        pltpu.make_async_copy(b.at[n], next_out.at[x], out_sem.at[n]).start()
        return carry

    lax.fori_loop(0, 2, advance, 0)
    for out, end, near, moving in ((to_west, 0, 0, MINUS), (to_east, 1, width - 1, PLUS)):
        slots = None
        for n, i in enumerate(moving):
            for t in range(tiles):
                out[n * tiles + t] = clean(b[end, i, :, pl.ds(t * TILE, TILE)])
            v = pltpu.roll(clean(strip2[i]), (4 * n - 4 * (near + 4)) % TILE, 1)
            slots = v if slots is None else jnp.where(at.slot == n, v, slots)
        out[NMOVE * tiles] = slots
    for n in range(2):
        pltpu.make_async_copy(b.at[n], next_out.at[n * (width - 1)], out_sem.at[n]).wait()


def advance_call(place, post, west, east, strip, kind, inner):
    width, _, depth, length = post.shape
    tiles = length // TILE
    f32 = jnp.float32
    vmem = pl.BlockSpec(memory_space=pltpu.VMEM)
    hbm = pl.BlockSpec(memory_space=pl.ANY)
    sends = NMOVE * tiles + 1
    return pl.pallas_call(
        advance_kernel,
        in_specs=[pl.BlockSpec(memory_space=pltpu.SMEM), hbm] + [vmem] * 4 + [hbm],
        out_specs=[hbm, vmem, vmem, vmem, vmem],
        out_shape=[
            jax.ShapeDtypeStruct((width, NP, depth, length), f32),
            jax.ShapeDtypeStruct((NP, depth, TILE), f32),
            jax.ShapeDtypeStruct((sends, depth, TILE), f32),
            jax.ShapeDtypeStruct((sends, depth, TILE), f32),
            jax.ShapeDtypeStruct((2 + 2 * tiles, depth, TILE), f32),
        ],
        scratch_shapes=[
            pltpu.VMEM((6, NP, depth, length), f32),
            pltpu.VMEM((SLOTS, depth, TILE), f32),
            pltpu.VMEM((NP, depth, length), f32),
            pltpu.VMEM((2, NP, depth, length), f32),
            pltpu.SemaphoreType.DMA((6,)),
            pltpu.SemaphoreType.DMA((2,)),
        ],
        input_output_aliases={6: 0},
        cost_estimate=cost(depth * 2 * length, 3),
        compiler_params=pltpu.CompilerParams(vmem_limit_bytes=24 * 2**20),
        name="advance",
    )(place, post, west, east, strip, kind, inner)


def close_faces(a, west, east, halo, kinds, at):
    tiles = a.shape[3] // TILE
    for face, edge, near, moving in (
        (west, at.west, 0, PLUS),
        (east, at.east, a.shape[0] - 1, MINUS),
    ):
        for t in range(tiles):
            solid = halo[2 + t if near == 0 else 2 + tiles + t] > 0.5
            span = slice(t * TILE, (t + 1) * TILE)
            for n, i in enumerate(moving):
                v = jnp.where(solid, MARK, face[n * tiles + t])
                outer = ghost(i, kinds[:, span]) if near == 0 else WEIGHTS[i]
                a[near, i, :, span] = jnp.where(edge, outer, v)


def settle_slab(b, x, near, strip, fout, hout, at):
    tiles = b.shape[3] // TILE
    solids = [marked(v) for v in pieces(b, near, 0, tiles)]
    for i in range(NP):
        buffer, index = (fout, i) if i < NF else (hout, i - NF)
        vs = pulled(lambda s, p: pieces(b, s - x + near, p, tiles), strip, x, i, at)
        backs = pieces(b, near, OPP[i], tiles)
        for t, (v, back) in enumerate(zip(vs, backs)):
            span = pl.ds(t * TILE, TILE)
            v = jnp.where(marked(v), back, v)
            buffer[index, :, span] = jnp.where(solids[t], buffer[index, :, span], v)


def settle_inner_kernel(
    place, fluid, heat, post, strip, fluid_out, heat_out, b, fout, hout, load_sem, fill_sem, out_sem
):
    width, depth = post.shape[0], post.shape[2]

    def load(x):
        return pltpu.make_async_copy(post.at[x], b.at[x], load_sem.at[x])

    def fill(x):
        return (
            pltpu.make_async_copy(fluid.at[:, :, x], fout.at[x], fill_sem.at[0, x]),
            pltpu.make_async_copy(heat.at[:, :, x], hout.at[x], fill_sem.at[1, x]),
        )

    def store(x):
        return (
            pltpu.make_async_copy(fout.at[x], fluid_out.at[:, :, x], out_sem.at[0, x]),
            pltpu.make_async_copy(hout.at[x], heat_out.at[:, :, x], out_sem.at[1, x]),
        )

    for x in range(width):
        load(x).start()
        if 0 < x < width - 1:
            for copy in fill(x):
                copy.start()
    at = Lanes(depth, width, place)
    load(0).wait()
    load(1).wait()

    def settle(x, carry):
        load(x + 1).wait()
        for copy in fill(x):
            copy.wait()
        settle_slab(b, x, x, strip, fout.at[x], hout.at[x], at)
        for copy in store(x):
            copy.start()
        return carry

    lax.fori_loop(1, width - 1, settle, 0)
    for x in range(1, width - 1):
        for copy in store(x):
            copy.wait()


def settle_inner_call(place, fluid, heat, post, strip):
    width, _, depth, length = post.shape
    f32 = jnp.float32
    vmem = pl.BlockSpec(memory_space=pltpu.VMEM)
    hbm = pl.BlockSpec(memory_space=pl.ANY)
    return pl.pallas_call(
        settle_inner_kernel,
        in_specs=[pl.BlockSpec(memory_space=pltpu.SMEM), hbm, hbm, hbm, vmem],
        out_specs=[hbm, hbm],
        out_shape=[
            jax.ShapeDtypeStruct(fluid.shape, f32),
            jax.ShapeDtypeStruct(heat.shape, f32),
        ],
        scratch_shapes=[
            pltpu.VMEM((width, NP, depth, length), f32),
            pltpu.VMEM((width, NF, depth, length), f32),
            pltpu.VMEM((width, NH, depth, length), f32),
            pltpu.SemaphoreType.DMA((width,)),
            pltpu.SemaphoreType.DMA((2, width)),
            pltpu.SemaphoreType.DMA((2, width)),
        ],
        cost_estimate=cost(depth * width * length, 3),
        compiler_params=pltpu.CompilerParams(vmem_limit_bytes=28 * 2**20),
        name="settle_inner",
    )(place, in_hbm(fluid), in_hbm(heat), post, strip)


def settle_kernel(
    place,
    fluid,
    heat,
    post,
    west,
    east,
    strip_in,
    halo,
    kind,
    fluid_in,
    heat_in,
    fluid_out,
    heat_out,
    b,
    strip,
    fout,
    hout,
    load_sem,
    fill_sem,
    out_sem,
):
    width, depth, length = post.shape[0], post.shape[2], post.shape[3]
    tiles = length // TILE
    loads = [
        pltpu.make_async_copy(post.at[x], b.at[n], load_sem.at[n]) for x, n in ends_of(width)
    ]
    for n in range(2):
        x = n * (width - 1)
        loads.append(pltpu.make_async_copy(fluid.at[:, :, x], fout.at[n], fill_sem.at[0, n]))
        loads.append(pltpu.make_async_copy(heat.at[:, :, x], hout.at[n], fill_sem.at[1, n]))
    for copy in loads:
        copy.start()
    at = Lanes(depth, width, place)
    for p in range(NP):
        strip[p] = strip_in[p]
    ends_w, ends_e = west[NMOVE * tiles], east[NMOVE * tiles]
    close_strip(strip, halo[1], ends_w, ends_e, halo[0] > 0.5, at, width)
    close_faces(b, west, east, halo, kind[...].astype(jnp.float32), at)
    for copy in loads:
        copy.wait()

    def store(n):
        x = n * (width - 1)
        return (
            pltpu.make_async_copy(fout.at[n], fluid_out.at[:, :, x], out_sem.at[0, n]),
            pltpu.make_async_copy(hout.at[n], heat_out.at[:, :, x], out_sem.at[1, n]),
        )

    def settle(n, carry):
        settle_slab(b, n * (width - 1), 1 + 3 * n, strip, fout.at[n], hout.at[n], at)
        for copy in store(n):
            copy.start()
        return carry

    lax.fori_loop(0, 2, settle, 0)
    for n in range(2):
        for copy in store(n):
            copy.wait()


def settle_call(place, fluid, heat, post, west, east, strip, halo, kind, inner):
    width, _, depth, length = post.shape
    f32 = jnp.float32
    vmem = pl.BlockSpec(memory_space=pltpu.VMEM)
    hbm = pl.BlockSpec(memory_space=pl.ANY)
    return pl.pallas_call(
        settle_kernel,
        in_specs=[pl.BlockSpec(memory_space=pltpu.SMEM), hbm, hbm, hbm] + [vmem] * 5 + [hbm] * 2,
        out_specs=[hbm, hbm],
        out_shape=[
            jax.ShapeDtypeStruct(fluid.shape, f32),
            jax.ShapeDtypeStruct(heat.shape, f32),
        ],
        scratch_shapes=[
            pltpu.VMEM((6, NP, depth, length), f32),
            pltpu.VMEM((NP, depth, TILE), f32),
            pltpu.VMEM((2, NF, depth, length), f32),
            pltpu.VMEM((2, NH, depth, length), f32),
            pltpu.SemaphoreType.DMA((6,)),
            pltpu.SemaphoreType.DMA((2, 2)),
            pltpu.SemaphoreType.DMA((2, 2)),
        ],
        input_output_aliases={9: 0, 10: 1},
        cost_estimate=cost(depth * 2 * length, 3),
        compiler_params=pltpu.CompilerParams(vmem_limit_bytes=24 * 2**20),
        name="settle",
    )(place, in_hbm(fluid), in_hbm(heat), post, west, east, strip, halo, kind, *inner)


def ring(v, axis, shift):
    n = lax.axis_size(axis)
    return lax.ppermute(v, axis, [(i, (i + shift) % n) for i in range(n)])


def swap(v, axis, odd):
    n = lax.axis_size(axis)
    pairs = [(i, i + 1) for i in range(odd, n - 1, 2)]
    return lax.ppermute(v, axis, pairs + [(j, i) for i, j in pairs])


def per_device(fluid, heat, solid_mask, inflow_type):
    ew, ns = lax.axis_index("ew"), lax.axis_index("ns")
    ew_size, ns_size = lax.axis_size("ew"), lax.axis_size("ns")
    place = [ew == 0, ew == ew_size - 1, ns == 0, ns == ns_size - 1, ns % 2 == 1]
    place = jnp.stack(place).astype(jnp.int32)
    own = column_call(fluid, heat, solid_mask, inflow_type)
    even, odd = swap(own, "ns", 0), swap(own, "ns", 1)
    post, to_west, to_east = collide_call(fluid, heat, solid_mask)
    strip, to_west, to_east = strip_call(
        solid_mask.shape[1], place, own, even, odd, to_west, to_east
    )
    west, east = ring(to_east, "ew", 1), ring(to_west, "ew", -1)
    inner = advance_inner_call(place, post, strip)
    post, strip2, to_west, to_east, halo = advance_call(
        place, post, west, east, strip, inflow_type, inner
    )
    west, east = ring(to_east, "ew", 1), ring(to_west, "ew", -1)
    inner = settle_inner_call(place, fluid, heat, post, strip2)
    return settle_call(
        place, fluid, heat, post, west, east, strip2, halo, inflow_type, inner
    )


def solution(mesh):
    return jax.shard_map(
        per_device,
        mesh=mesh,
        in_specs=(
            P(None, None, "ew", "ns"),
            P(None, None, "ew", "ns"),
            P(None, "ew", "ns"),
            P(None, "ns"),
        ),
        out_specs=(P(None, None, "ew", "ns"), P(None, None, "ew", "ns")),
        check_vma=False,
    )
```

```python
import functools
import math

import jax
import jax.numpy as jnp
from jax import lax
from jax.experimental import pallas as pl
from jax.experimental.pallas import tpu as pltpu
from jax.sharding import PartitionSpec as P

FLUID_DIRS = [
    (0, 0, 0),
    (1, 0, 0),
    (-1, 0, 0),
    (0, 1, 0),
    (0, -1, 0),
    (0, 0, 1),
    (0, 0, -1),
    (1, 1, 0),
    (-1, -1, 0),
    (1, -1, 0),
    (-1, 1, 0),
    (1, 0, 1),
    (-1, 0, -1),
    (1, 0, -1),
    (-1, 0, 1),
    (0, 1, 1),
    (0, -1, -1),
    (0, 1, -1),
    (0, -1, 1),
]
DIRS = FLUID_DIRS + FLUID_DIRS[:7]
NF, NH = 19, 7
NP = NF + NH
OPP = [
    (FLUID_DIRS.index((-c[0], -c[1], -c[2])) + (0 if i < NF else NF)) for i, c in enumerate(DIRS)
]
WEIGHTS = (
    [1.0 / 3.0] + [1.0 / 18.0] * 6 + [1.0 / 36.0] * 12 + [0.25] + [0.125] * 6
)
PLUS = [i for i, c in enumerate(DIRS) if c[0] == 1]
MINUS = [i for i, c in enumerate(DIRS) if c[0] == -1]
TAU = 0.6
TAU_HEAT = 0.8
COUPLING = 0.02
INFLOW_SPEED = 0.08
COOLING = 0.2
MARK = float("nan")
MASK, KIND = NP, NP + 1
SLOTS = NP + 2
NMOVE = len(PLUS)
NFACE = NMOVE + 1
TILE = 128
GROUP = 4
GROUPS = SLOTS // GROUP
PITCH = TILE // GROUP


def collided(f, solid):
    pairs = {k: (f[k] + f[k + 1], f[k] - f[k + 1]) for k in range(1, NF, 2)}
    s = {k: v[0] for k, v in pairs.items()}
    d = {k: v[1] for k, v in pairs.items()}
    rho = (f[0] + (s[1] + s[3])) + ((s[5] + s[7]) + (s[9] + s[11])) + ((s[13] + s[15]) + s[17])
    mx = (d[1] + d[7]) + (d[9] + (d[11] + d[13]))
    my = (d[3] + d[7]) + ((d[15] - d[9]) + d[17])
    mz = (d[5] + d[11]) + ((d[15] - d[13]) - d[17])
    g = f[NF:]
    hp = [(g[k] + g[k + 1]) for k in (1, 3, 5)]
    warm = (g[0] + hp[0]) + (hp[1] + hp[2])
    inv = 1.0 / rho
    ux, uy, uz = mx * inv, my * inv, mz * inv
    lifted = uz + TAU * COUPLING * (warm - 1.0)
    root = math.sqrt(4.5)
    ax, ay, az = ux * root, uy * root, lifted * root
    base = 1.0 - (ax * ax + ay * ay + az * az) * (1.0 / 3.0)
    keep = 1.0 - 1.0 / TAU
    r = jnp.where(solid, MARK, rho * (1.0 / TAU))
    r18, r36 = r * (1.0 / 18.0), r * (1.0 / 36.0)
    o18, o36 = r18 * (3.0 / root), r36 * (3.0 / root)
    out = [None] * NP
    out[0] = keep * f[0] + (r * (1.0 / 3.0)) * base
    along = {
        1: ax,
        3: ay,
        5: az,
        7: ax + ay,
        9: ax - ay,
        11: ax + az,
        13: ax - az,
        15: ay + az,
        17: ay - az,
    }
    for k, e in along.items():
        w, o = (r18, o18) if k < 7 else (r36, o36)
        even = w * (base + e * e)
        odd = o * e
        out[k] = keep * f[k] + (even + odd)
        out[k + 1] = keep * f[k + 1] + (even - odd)
    hkeep = 1.0 - 1.0 / TAU_HEAT
    t8 = jnp.where(solid, MARK, warm * (0.125 / TAU_HEAT))
    out[NF] = hkeep * g[0] + (t8 + t8)
    t2 = t8 * 4.0
    for k, u in ((1, ux), (3, uy), (5, uz)):
        odd = t2 * u
        out[NF + k] = hkeep * g[k] + (t8 + odd)
        out[NF + k + 1] = hkeep * g[k + 1] + (t8 - odd)
    return out


def ghost(i, kind):
    u = (INFLOW_SPEED * 0.5) * kind
    cx = DIRS[i][0]
    if i < NF:
        return WEIGHTS[i] * (1.0 + 3.0 * cx * u + (4.5 * cx * cx - 1.5) * (u * u))
    return WEIGHTS[i] * (1.0 - COOLING * kind) * (1.0 + 4.0 * cx * u)


def marked(v):
    return v != v


def clean(v):
    return jnp.where(marked(v), 0.0, v)


def collide_slab(x, before, solid, post):
    depth, length = post.shape[2], post.shape[3]
    for z in range(0, depth, 8):
        for t in range(length // TILE):
            part, span = pl.ds(z, 8), pl.ds(t * TILE, TILE)
            f = [before[x, i, part, span] for i in range(NP)]
            for i, v in enumerate(collided(f, solid[x, part, span] > 0)):
                post[x, i, part, span] = v


def collide_kernel(before, solid, post, west, east):
    width, length = post.shape[0], post.shape[3]
    tiles = length // TILE

    def collide(x, carry):
        collide_slab(x, before, solid, post)
        return carry

    lax.fori_loop(0, width, collide, 0)
    for face, near, moving in ((west, 0, MINUS), (east, width - 1, PLUS)):
        for t in range(tiles):
            span = pl.ds(t * TILE, TILE)
            for n, i in enumerate(moving):
                face[n * tiles + t] = clean(post[near, i, :, span])
            face[NMOVE * tiles + t] = jnp.where(solid[near, :, span] > 0, 1.0, 0.0)


def collide_call(before, solid):
    width, _, depth, length = before.shape
    face = jax.ShapeDtypeStruct((NFACE * (length // TILE), depth, TILE), jnp.float32)
    vmem = pl.BlockSpec(memory_space=pltpu.VMEM)
    return pl.pallas_call(
        collide_kernel,
        in_specs=[vmem, vmem],
        out_specs=[vmem, vmem, vmem],
        out_shape=[jax.ShapeDtypeStruct(before.shape, jnp.float32), face, face],
        cost_estimate=cost(depth * width * length, 2),
        compiler_params=pltpu.CompilerParams(vmem_limit_bytes=16 * 2**20),
        name="collide",
    )(before, solid)


def column_kernel(place, fluid, heat, mask, kind, packed, before, solid, kinds, total, sem, kind_sem):
    width, depth, length = solid.shape
    shape = (depth, TILE)
    lanes = lax.broadcasted_iota(jnp.int32, shape, 1)
    start, stop = lanes < 2, lanes >= TILE - 2
    first, last = pl.ds(0, TILE), pl.ds(length - TILE, TILE)

    def fetch(x):
        return (
            pltpu.make_async_copy(mask.at[:, x], solid.at[x], sem.at[x, 0]),
            pltpu.make_async_copy(fluid.at[:, :, x], before.at[x, pl.ds(0, NF)], sem.at[x, 1]),
            pltpu.make_async_copy(heat.at[:, :, x], before.at[x, pl.ds(NF, NH)], sem.at[x, 2]),
        )

    for x in range(width):
        for copy in fetch(x):
            copy.start()
    fetch_kind = pltpu.make_async_copy(kind, kinds, kind_sem)
    fetch_kind.start()
    for p in range(SLOTS):
        total[p] = jnp.zeros(shape, jnp.float32)
    fetch_kind.wait()
    k = [kinds[:, first].astype(jnp.float32), kinds[:, last].astype(jnp.float32)]
    kind_ends = jnp.where(stop, k[1], jnp.where(start, k[0], 0.0))

    def gather(x, carry):
        for copy in fetch(x):
            copy.wait()
        shift = x * 4 + 2
        for i in range(NP):
            ends = jnp.where(stop, before[x, i, :, last], before[x, i, :, first])
            ends = jnp.where(start | stop, ends, 0.0)
            total[i] = total[i] + pltpu.roll(ends, shift, 1)
        ends = jnp.where(stop, solid[x, :, last], solid[x, :, first]).astype(jnp.float32)
        ends = jnp.where(start | stop, ends, 0.0)
        total[MASK] = total[MASK] + pltpu.roll(ends, shift, 1)
        total[KIND] = total[KIND] + pltpu.roll(kind_ends, shift, 1)
        return carry

    lax.fori_loop(0, width, gather, 0)
    for z in range(0, depth, 8):
        part = pl.ds(z, 8)
        f = [total[i, part] for i in range(NP)]
        filled = total[MASK, part] > 0.5
        idle = filled | (lanes[z : z + 8] >= 4 * width)
        out = [jnp.where(idle, 0.0, v) for v in collided(f, filled)]
        out += [total[MASK, part], total[KIND, part]]
        for group in range(GROUPS):
            v = out[group * GROUP]
            for k in range(1, GROUP):
                v = v + pltpu.roll(out[group * GROUP + k], k * PITCH, 1)
            packed[group, part] = v


def column_call(place, fluid, heat, mask, kind):
    depth, width, length = mask.shape
    f32 = jnp.float32
    vmem = pl.BlockSpec(memory_space=pltpu.VMEM)
    hbm = pl.BlockSpec(memory_space=pl.ANY)
    return pl.pallas_call(
        column_kernel,
        in_specs=[pl.BlockSpec(memory_space=pltpu.SMEM)] + [hbm] * 4,
        out_specs=[vmem] * 3,
        out_shape=[
            jax.ShapeDtypeStruct((GROUPS, depth, TILE), f32),
            jax.ShapeDtypeStruct((width, NP, depth, length), f32),
            jax.ShapeDtypeStruct((width, depth, length), jnp.int32),
        ],
        scratch_shapes=[
            pltpu.VMEM((depth, length), jnp.int32),
            pltpu.VMEM((SLOTS, depth, TILE), f32),
            pltpu.SemaphoreType.DMA((width, 3)),
            pltpu.SemaphoreType.DMA,
        ],
        cost_estimate=cost(depth * width * length, 2),
        compiler_params=pltpu.CompilerParams(vmem_limit_bytes=16 * 2**20),
        name="columns",
    )(place, *[in_hbm(v) for v in (fluid, heat, mask, kind)])


def in_hbm(v):
    return pltpu.with_memory_space_constraint(v, pltpu.HBM)


def cost(cells, passes):
    return pl.CostEstimate(
        flops=300 * cells * passes, bytes_accessed=4 * NP * cells * passes, transcendentals=0
    )


class Lanes:
    def __init__(self, depth, place):
        shape = (depth, TILE)
        lane = lax.broadcasted_iota(jnp.int32, shape, 1)
        level = lax.broadcasted_iota(jnp.int32, shape, 0)
        self.side, self.slot, self.j = lane // 64, (lane % 64) // 4, lane % 4
        self.ground, self.top = level == 0, level == depth - 1
        self.first, self.last = lane == 0, lane == TILE - 1
        self.west, self.east = place[0] == 1, place[1] == 1
        low = (place[2] == 1) & (self.side == 0) & (self.j < 2)
        high = (place[3] == 1) & (self.side == 1) & (self.j >= 2)
        self.beyond_y = low | high


def strip_kernel(width, place, own, even, odd, after, strip, to_west, to_east):
    depth = own.shape[1]
    at = Lanes(depth, place)
    flip = place[4] == 1
    slots_w = [None] * NFACE
    slots_e = [None] * NFACE
    near_j = at.j < 2
    for group in range(GROUPS):
        o = own[group]
        above = jnp.where(flip, odd[group], even[group])
        below = jnp.where(flip, even[group], odd[group])
        low, high = jnp.where(near_j, below, o), jnp.where(near_j, o, above)
        for k in range(GROUP):
            p = group * GROUP + k
            v = jnp.where(
                at.side == 0,
                pltpu.roll(low, (16 - k * PITCH) % TILE, 1),
                pltpu.roll(high, (80 - k * PITCH) % TILE, 1),
            )
            strip[p] = v
            if p in MINUS or p == MASK:
                n = NMOVE if p == MASK else MINUS.index(p)
                slots_w[n] = pltpu.roll(v, (4 * n - 16) % TILE, 1)
            if p in PLUS or p == MASK:
                n = NMOVE if p == MASK else PLUS.index(p)
                slots_e[n] = pltpu.roll(v, (4 * n - 12 - 4 * width) % TILE, 1)
    for out, slots in ((to_west, slots_w), (to_east, slots_e)):
        total = jnp.zeros_like(slots[0])
        for n, v in enumerate(slots):
            total = jnp.where(at.slot == n, v, total)
        out[...] = total
    solid = strip[MASK] > 0.5
    for i in range(NP):
        strip[i] = jnp.where(at.beyond_y, WEIGHTS[i], jnp.where(solid, MARK, strip[i]))


def strip_call(width, place, own, even, odd, after):
    _, depth, _ = own.shape
    f32 = jnp.float32
    vmem = pl.BlockSpec(memory_space=pltpu.VMEM)
    return pl.pallas_call(
        functools.partial(strip_kernel, width),
        in_specs=[pl.BlockSpec(memory_space=pltpu.SMEM)]
        + [vmem] * 3
        + [pl.BlockSpec(memory_space=pl.ANY)],
        out_specs=[vmem, vmem, vmem],
        out_shape=[
            jax.ShapeDtypeStruct((SLOTS, depth, TILE), f32),
            jax.ShapeDtypeStruct((depth, TILE), f32),
            jax.ShapeDtypeStruct((depth, TILE), f32),
        ],
        compiler_params=pltpu.CompilerParams(vmem_limit_bytes=8 * 2**20),
        name="strips",
    )(place, own, even, odd, after)


def raised(v, i, at):
    depth = v.shape[0]
    cz = DIRS[i][2]
    if cz == 1:
        return jnp.where(at.ground, MARK, pltpu.roll(v, 1, 0))
    if cz == -1:
        return jnp.where(at.top, WEIGHTS[i], pltpu.roll(v, depth - 1, 0))
    return v


def pieces(ref, index, i, tiles):
    return [ref[index, i, :, pl.ds(t * TILE, TILE)] for t in range(tiles)]


def turned(v, shift):
    shift = shift % TILE if isinstance(shift, int) else lax.rem(shift + 4 * TILE, TILE)
    return pltpu.roll(v, shift, 1)


def pulled(cells, cols, x, i, at):
    cx, cy, _ = DIRS[i]
    source = cells(x - cx, i)
    if cy:
        moved = [turned(v, cy) for v in source]
        lane = (x - cx + 4) * 4
        if cy == 1:
            before = [turned(cols[i], -1 - lane)] + moved[:-1]
            source = [jnp.where(at.first, p, v) for p, v in zip(before, moved)]
        else:
            after = moved[1:] + [turned(cols[i], TILE - 1 - (64 + lane + 2))]
            source = [jnp.where(at.last, n, v) for n, v in zip(after, moved)]
    return [raised(v, i, at) for v in source]


def close_strip(strip, kinds, from_west, from_east, solid, at, width):
    kind = jnp.where(at.beyond_y, 0.0, kinds)
    for face, edge, slot, moving in (
        (from_west, at.west, 3, PLUS),
        (from_east, at.east, 4 + width, MINUS),
    ):
        here = at.slot == slot
        for n, i in enumerate(moving):
            v = pltpu.roll(face, (4 * slot - 4 * n) % TILE, 1)
            v = jnp.where(solid, MARK, v)
            v = jnp.where(at.beyond_y, WEIGHTS[i], v)
            v = jnp.where(edge, ghost(i, kind) if slot == 3 else WEIGHTS[i], v)
            strip[i] = jnp.where(here, v, strip[i])


def layers(ref, tiles, halo=None):
    def cells(x, i):
        if halo is not None and isinstance(x, int) and not 0 <= x < ref.shape[0]:
            return pieces(halo, 0 if x < 0 else 1, i, tiles)
        return pieces(ref, x, i, tiles)

    return cells


def advance_slab(cells, x, strip, fresh, out, at):
    depth, length = fresh.shape[1], fresh.shape[2]
    tiles = length // TILE
    for i in range(NP):
        vs = pulled(cells, strip, x, i, at)
        for t, (v, back) in enumerate(zip(vs, cells(x, OPP[i]))):
            fresh[i, :, pl.ds(t * TILE, TILE)] = jnp.where(marked(v), back, v)
    own = cells(x, 0)
    for z in range(0, depth, 8):
        for t in range(tiles):
            part, span = pl.ds(z, 8), pl.ds(t * TILE, TILE)
            f = [fresh[i, part, span] for i in range(NP)]
            solid = marked(own[t][z : z + 8])
            for i, v in enumerate(collided(f, solid)):
                out[x, i, part, span] = v


def advance_inner_kernel(low, high, place, post, strip, *refs):
    out, fresh = refs[-2:]
    depth, length = post.shape[2], post.shape[3]
    at = Lanes(depth, place)
    cells = layers(post, length // TILE)

    def advance(x, carry):
        advance_slab(cells, x, strip, fresh, out, at)
        return carry

    lax.fori_loop(low, high, advance, 0)


def advance_inner_call(place, post, strip, low, high, *others):
    width, _, depth, length = post.shape
    f32 = jnp.float32
    vmem = pl.BlockSpec(memory_space=pltpu.VMEM)
    return pl.pallas_call(
        functools.partial(advance_inner_kernel, low, high),
        in_specs=[pl.BlockSpec(memory_space=pltpu.SMEM)] + [vmem] * (2 + len(others)),
        out_specs=vmem,
        out_shape=jax.ShapeDtypeStruct((width, NP, depth, length), f32),
        scratch_shapes=[pltpu.VMEM((NP, depth, length), f32)],
        input_output_aliases={3: 0} if others else {},
        cost_estimate=cost(depth * (high - low) * length, 4),
        compiler_params=pltpu.CompilerParams(vmem_limit_bytes=16 * 2**20),
        name="advance_inner",
    )(place, post, strip, *others)


def advance_kernel(
    place,
    post,
    west,
    east,
    strip_in,
    strip_w,
    strip_e,
    kind,
    next_in,
    next_out,
    strip2,
    to_west,
    to_east,
    halo,
    a,
    strip,
    fresh,
):
    width, depth, length = post.shape[0], post.shape[2], post.shape[3]
    tiles = length // TILE
    at = Lanes(depth, place)
    for p in range(SLOTS):
        strip[p] = strip_in[p]
    ends_w, ends_e = strip_w[...], strip_e[...]
    ends = jnp.where(
        at.slot == 3,
        pltpu.roll(ends_w, (12 - 4 * NMOVE) % TILE, 1),
        pltpu.roll(ends_e, (16 + 4 * width - 4 * NMOVE) % TILE, 1),
    )
    kind_end = pltpu.roll(strip[KIND], TILE - 4, 1)
    close_strip(strip, kind_end, ends_w, ends_e, ends > 0.5, at, width)
    halo[0], halo[1] = ends, kind_end
    for n, face in ((2, west), (2 + tiles, east)):
        for t in range(tiles):
            halo[n + t] = face[NMOVE * tiles + t]
    kinds = kind[...].astype(jnp.float32)
    close_faces(a, west, east, halo, kinds, at)

    for i in range(NP):
        cx, cy, _ = DIRS[i]
        v = strip[i]
        if cx or cy:
            v = pltpu.roll(v, (4 * cx + cy) % TILE, 1)
        v = raised(v, i, at)
        fresh[i, :, pl.ds(0, TILE)] = jnp.where(marked(v), strip[OPP[i]], v)
    for z in range(0, depth, 8):
        part = pl.ds(z, 8)
        f = [fresh[i, part, pl.ds(0, TILE)] for i in range(NP)]
        outside = at.beyond_y[z : z + 8]
        for i, v in enumerate(collided(f, marked(strip[0, part]))):
            strip2[i, part] = jnp.where(outside, WEIGHTS[i], v)

    cells = layers(post, tiles, a)
    for x in (0, width - 1):
        advance_slab(cells, x, strip, fresh, next_out, at)
    for out, near, moving in ((to_west, 0, MINUS), (to_east, width - 1, PLUS)):
        slots = None
        for n, i in enumerate(moving):
            for t in range(tiles):
                out[n * tiles + t] = clean(next_out[near, i, :, pl.ds(t * TILE, TILE)])
            v = pltpu.roll(clean(strip2[i]), (4 * n - 4 * (near + 4)) % TILE, 1)
            slots = v if slots is None else jnp.where(at.slot == n, v, slots)
        out[NMOVE * tiles] = slots


def advance_call(place, post, west, east, strip, strip_w, strip_e, kind, inner):
    width, _, depth, length = post.shape
    tiles = length // TILE
    f32 = jnp.float32
    vmem = pl.BlockSpec(memory_space=pltpu.VMEM)
    sends = NMOVE * tiles + 1
    return pl.pallas_call(
        advance_kernel,
        in_specs=[pl.BlockSpec(memory_space=pltpu.SMEM)] + [vmem] * 8,
        out_specs=[vmem] * 5,
        out_shape=[
            jax.ShapeDtypeStruct((width, NP, depth, length), f32),
            jax.ShapeDtypeStruct((NP, depth, TILE), f32),
            jax.ShapeDtypeStruct((sends, depth, TILE), f32),
            jax.ShapeDtypeStruct((sends, depth, TILE), f32),
            jax.ShapeDtypeStruct((2 + 2 * tiles, depth, TILE), f32),
        ],
        scratch_shapes=[
            pltpu.VMEM((2, NP, depth, length), f32),
            pltpu.VMEM((SLOTS, depth, TILE), f32),
            pltpu.VMEM((NP, depth, length), f32),
        ],
        input_output_aliases={8: 0},
        cost_estimate=cost(depth * 2 * length, 3),
        compiler_params=pltpu.CompilerParams(vmem_limit_bytes=24 * 2**20),
        name="advance",
    )(place, post, west, east, strip, strip_w, strip_e, kind, inner)


def close_faces(a, west, east, halo, kinds, at):
    tiles = a.shape[3] // TILE
    for face, edge, near, moving in (
        (west, at.west, 0, PLUS),
        (east, at.east, 1, MINUS),
    ):
        for t in range(tiles):
            solid = halo[2 + t if near == 0 else 2 + tiles + t] > 0.5
            span = slice(t * TILE, (t + 1) * TILE)
            for n, i in enumerate(moving):
                v = jnp.where(solid, MARK, face[n * tiles + t])
                outer = ghost(i, kinds[:, span]) if near == 0 else WEIGHTS[i]
                a[near, i, :, span] = jnp.where(edge, outer, v)


def settle_slab(cells, x, strip, before, out, at):
    solids = [marked(v) for v in cells(x, 0)]
    for i in range(NP):
        vs = pulled(cells, strip, x, i, at)
        for t, (v, back) in enumerate(zip(vs, cells(x, OPP[i]))):
            span = pl.ds(t * TILE, TILE)
            v = jnp.where(marked(v), back, v)
            out[i, :, span] = jnp.where(solids[t], before[x, i, :, span], v)


def stores(buffer, fluid_out, heat_out, x, sem):
    return (
        pltpu.make_async_copy(buffer.at[pl.ds(0, NF)], fluid_out.at[:, :, x], sem.at[0]),
        pltpu.make_async_copy(buffer.at[pl.ds(NF, NH)], heat_out.at[:, :, x], sem.at[1]),
    )


def settle_inner_kernel(place, before, post, strip, fluid_out, heat_out, buffer, sem):
    width, depth, length = post.shape[0], post.shape[2], post.shape[3]
    at = Lanes(depth, place)
    cells = layers(post, length // TILE)

    def settle(x, carry):
        settle_slab(cells, x, strip, before, buffer.at[x], at)
        for copy in stores(buffer.at[x], fluid_out, heat_out, x, sem.at[x]):
            copy.start()
        return carry

    lax.fori_loop(1, width - 1, settle, 0)
    for x in range(1, width - 1):
        for copy in stores(buffer.at[x], fluid_out, heat_out, x, sem.at[x]):
            copy.wait()


def settle_inner_call(place, before, post, strip, outs):
    width, _, depth, length = post.shape
    vmem = pl.BlockSpec(memory_space=pltpu.VMEM)
    hbm = pl.BlockSpec(memory_space=pl.ANY)
    return pl.pallas_call(
        settle_inner_kernel,
        in_specs=[pl.BlockSpec(memory_space=pltpu.SMEM)] + [vmem] * 3,
        out_specs=[hbm, hbm],
        out_shape=[jax.ShapeDtypeStruct(v.shape, v.dtype) for v in outs],
        scratch_shapes=[
            pltpu.VMEM((width, NP, depth, length), jnp.float32),
            pltpu.SemaphoreType.DMA((width, 2)),
        ],
        cost_estimate=cost(depth * width * length, 3),
        compiler_params=pltpu.CompilerParams(vmem_limit_bytes=24 * 2**20),
        name="settle_inner",
    )(place, before, post, strip)


def settle_kernel(
    place,
    before,
    post,
    west,
    east,
    strip_in,
    halo,
    kind,
    fluid_in,
    heat_in,
    fluid_out,
    heat_out,
    b,
    strip,
    buffer,
    sem,
):
    width, depth, length = post.shape[0], post.shape[2], post.shape[3]
    tiles = length // TILE
    at = Lanes(depth, place)
    for p in range(NP):
        strip[p] = strip_in[p]
    ends_w, ends_e = west[NMOVE * tiles], east[NMOVE * tiles]
    close_strip(strip, halo[1], ends_w, ends_e, halo[0] > 0.5, at, width)
    close_faces(b, west, east, halo, kind[...].astype(jnp.float32), at)
    cells = layers(post, tiles, b)
    ends = ((0, 0), (1, width - 1))
    for n, x in ends:
        settle_slab(cells, x, strip, before, buffer.at[n], at)
        for copy in stores(buffer.at[n], fluid_out, heat_out, x, sem.at[n]):
            copy.start()
    for n, x in ends:
        for copy in stores(buffer.at[n], fluid_out, heat_out, x, sem.at[n]):
            copy.wait()


def settle_call(place, before, post, west, east, strip, halo, kind, inner):
    _, _, depth, length = post.shape
    f32 = jnp.float32
    vmem = pl.BlockSpec(memory_space=pltpu.VMEM)
    hbm = pl.BlockSpec(memory_space=pl.ANY)
    return pl.pallas_call(
        settle_kernel,
        in_specs=[pl.BlockSpec(memory_space=pltpu.SMEM)] + [vmem] * 7 + [hbm] * 2,
        out_specs=[hbm, hbm],
        out_shape=[jax.ShapeDtypeStruct(v.shape, v.dtype) for v in inner],
        scratch_shapes=[
            pltpu.VMEM((2, NP, depth, length), f32),
            pltpu.VMEM((NP, depth, TILE), f32),
            pltpu.VMEM((2, NP, depth, length), f32),
            pltpu.SemaphoreType.DMA((2, 2)),
        ],
        input_output_aliases={8: 0, 9: 1},
        cost_estimate=cost(depth * 2 * length, 3),
        compiler_params=pltpu.CompilerParams(vmem_limit_bytes=24 * 2**20),
        name="settle",
    )(place, before, post, west, east, strip, halo, kind, *inner)


def ring(v, axis, shift):
    n = lax.axis_size(axis)
    return lax.ppermute(v, axis, [(i, (i + shift) % n) for i in range(n)])


def swap(v, axis, odd):
    n = lax.axis_size(axis)
    pairs = [(i, i + 1) for i in range(odd, n - 1, 2)]
    return lax.ppermute(v, axis, pairs + [(j, i) for i, j in pairs])


def per_device(fluid, heat, solid_mask, inflow_type):
    ew, ns = lax.axis_index("ew"), lax.axis_index("ns")
    ew_size, ns_size = lax.axis_size("ew"), lax.axis_size("ns")
    place = [ew == 0, ew == ew_size - 1, ns == 0, ns == ns_size - 1, ns % 2 == 1]
    place = jnp.stack(place).astype(jnp.int32)
    width = solid_mask.shape[1]
    own, before, solid = column_call(place, fluid, heat, solid_mask, inflow_type)
    even = swap(own, "ns", 0)
    odd = swap(own, "ns", 1)
    post, to_west, to_east = collide_call(before, solid)
    west, east = ring(to_east, "ew", 1), ring(to_west, "ew", -1)
    strip, to_west, to_east = strip_call(width, place, own, even, odd, to_west)
    strip_w, strip_e = ring(to_east, "ew", 1), ring(to_west, "ew", -1)
    middle = width // 2
    done = advance_inner_call(place, post, strip, 1, middle)
    done, strip2, to_west, to_east, halo = advance_call(
        place, post, west, east, strip, strip_w, strip_e, inflow_type, done
    )
    west, east = ring(to_east, "ew", 1), ring(to_west, "ew", -1)
    post = advance_inner_call(place, post, strip, middle, width - 1, done)
    inner = settle_inner_call(place, before, post, strip2, (fluid, heat))
    return settle_call(place, before, post, west, east, strip2, halo, inflow_type, inner)


def solution(mesh):
    return jax.shard_map(
        per_device,
        mesh=mesh,
        in_specs=(
            P(None, None, "ew", "ns"),
            P(None, None, "ew", "ns"),
            P(None, "ew", "ns"),
            P(None, "ns"),
        ),
        out_specs=(P(None, None, "ew", "ns"), P(None, None, "ew", "ns")),
        check_vma=False,
    )
```

```python
import functools
import math

import jax
import jax.numpy as jnp
from jax import lax
from jax.experimental import pallas as pl
from jax.experimental.pallas import tpu as pltpu
from jax.sharding import PartitionSpec as P

FLUID_DIRS = [
    (0, 0, 0),
    (1, 0, 0),
    (-1, 0, 0),
    (0, 1, 0),
    (0, -1, 0),
    (0, 0, 1),
    (0, 0, -1),
    (1, 1, 0),
    (-1, -1, 0),
    (1, -1, 0),
    (-1, 1, 0),
    (1, 0, 1),
    (-1, 0, -1),
    (1, 0, -1),
    (-1, 0, 1),
    (0, 1, 1),
    (0, -1, -1),
    (0, 1, -1),
    (0, -1, 1),
]
DIRS = FLUID_DIRS + FLUID_DIRS[:7]
NF, NH = 19, 7
NP = NF + NH
OPP = [
    (FLUID_DIRS.index((-c[0], -c[1], -c[2])) + (0 if i < NF else NF)) for i, c in enumerate(DIRS)
]
WEIGHTS = (
    [1.0 / 3.0] + [1.0 / 18.0] * 6 + [1.0 / 36.0] * 12 + [0.25] + [0.125] * 6
)
PLUS = [i for i, c in enumerate(DIRS) if c[0] == 1]
MINUS = [i for i, c in enumerate(DIRS) if c[0] == -1]
TAU = 0.6
TAU_HEAT = 0.8
COUPLING = 0.02
INFLOW_SPEED = 0.08
COOLING = 0.2
MARK = float("nan")
MASK, KIND = NP, NP + 1
SLOTS = NP + 2
NMOVE = len(PLUS)
NFACE = NMOVE + 1
TILE = 128
GROUP = 4
GROUPS = SLOTS // GROUP
PITCH = TILE // GROUP
MIDDLE = 3


def collided(f, solid):
    pairs = {k: (f[k] + f[k + 1], f[k] - f[k + 1]) for k in range(1, NF, 2)}
    s = {k: v[0] for k, v in pairs.items()}
    d = {k: v[1] for k, v in pairs.items()}
    rho = (f[0] + (s[1] + s[3])) + ((s[5] + s[7]) + (s[9] + s[11])) + ((s[13] + s[15]) + s[17])
    mx = (d[1] + d[7]) + (d[9] + (d[11] + d[13]))
    my = (d[3] + d[7]) + ((d[15] - d[9]) + d[17])
    mz = (d[5] + d[11]) + ((d[15] - d[13]) - d[17])
    g = f[NF:]
    hp = [(g[k] + g[k + 1]) for k in (1, 3, 5)]
    warm = (g[0] + hp[0]) + (hp[1] + hp[2])
    inv = 1.0 / rho
    ux, uy, uz = mx * inv, my * inv, mz * inv
    lifted = uz + TAU * COUPLING * (warm - 1.0)
    root = math.sqrt(4.5)
    ax, ay, az = ux * root, uy * root, lifted * root
    base = 1.0 - (ax * ax + ay * ay + az * az) * (1.0 / 3.0)
    keep = 1.0 - 1.0 / TAU
    r = jnp.where(solid, MARK, rho * (1.0 / TAU))
    r18, r36 = r * (1.0 / 18.0), r * (1.0 / 36.0)
    o18, o36 = r18 * (3.0 / root), r36 * (3.0 / root)
    out = [None] * NP
    out[0] = keep * f[0] + (r * (1.0 / 3.0)) * base
    along = {
        1: ax,
        3: ay,
        5: az,
        7: ax + ay,
        9: ax - ay,
        11: ax + az,
        13: ax - az,
        15: ay + az,
        17: ay - az,
    }
    for k, e in along.items():
        w, o = (r18, o18) if k < 7 else (r36, o36)
        even = w * (base + e * e)
        odd = o * e
        out[k] = keep * f[k] + (even + odd)
        out[k + 1] = keep * f[k + 1] + (even - odd)
    hkeep = 1.0 - 1.0 / TAU_HEAT
    t8 = jnp.where(solid, MARK, warm * (0.125 / TAU_HEAT))
    out[NF] = hkeep * g[0] + (t8 + t8)
    t2 = t8 * 4.0
    for k, u in ((1, ux), (3, uy), (5, uz)):
        odd = t2 * u
        out[NF + k] = hkeep * g[k] + (t8 + odd)
        out[NF + k + 1] = hkeep * g[k + 1] + (t8 - odd)
    return out


def ghost(i, kind):
    u = (INFLOW_SPEED * 0.5) * kind
    cx = DIRS[i][0]
    if i < NF:
        return WEIGHTS[i] * (1.0 + 3.0 * cx * u + (4.5 * cx * cx - 1.5) * (u * u))
    return WEIGHTS[i] * (1.0 - COOLING * kind) * (1.0 + 4.0 * cx * u)


def marked(v):
    return v != v


def clean(v):
    return jnp.where(marked(v), 0.0, v)


def collide_slab(x, before, solid, post):
    width, _, depth, length = post.shape
    for z in range(0, depth, 8):
        cells = pl.ds(z * width + x, 8, stride=width)
        for t in range(length // TILE):
            f = [before[t, i, cells] for i in range(NP)]
            for i, v in enumerate(collided(f, solid[t, cells] > 0)):
                post[x, i, pl.ds(z, 8), pl.ds(t * TILE, TILE)] = v


def collide_kernel(before, solid, ends, post):
    def collide(x, carry):
        collide_slab(x, before, solid, post)
        return carry

    lax.fori_loop(1, post.shape[0] - 1, collide, 0)


def collide_call(before, solid, ends):
    vmem = pl.BlockSpec(memory_space=pltpu.VMEM)
    return pl.pallas_call(
        collide_kernel,
        in_specs=[vmem] * 3,
        out_specs=vmem,
        out_shape=jax.ShapeDtypeStruct(ends.shape, jnp.float32),
        input_output_aliases={2: 0},
        cost_estimate=cost(ends.size // NP, 2),
        compiler_params=pltpu.CompilerParams(vmem_limit_bytes=16 * 2**20),
        name="collide",
    )(before, solid, ends)


def column_kernel(
    width,
    fluid,
    heat,
    mask,
    kind,
    packed,
    before,
    solid,
    post,
    west,
    east,
    kinds,
    sem,
    kind_sem,
):
    tiles, _, count, _ = before.shape
    rows = 8
    lanes = lax.broadcasted_iota(jnp.int32, (rows, TILE), 1)
    stop = lanes >= TILE - 2
    middle = (lanes >= 2) & (lanes < TILE - 2)
    block = rows * width

    def fetch(n):
        part = pl.ds(n * block, block)
        copies = []
        for t in range(tiles):
            span = pl.ds(t * TILE, TILE)
            for k, (source, target) in enumerate(
                (
                    (mask.at[part, span], solid.at[t, part]),
                    (fluid.at[:, part, span], before.at[t, pl.ds(0, NF), part]),
                    (heat.at[:, part, span], before.at[t, pl.ds(NF, NH), part]),
                )
            ):
                copies.append(pltpu.make_async_copy(source, target, sem.at[n, t, k]))
        return copies

    fetch_kind = pltpu.make_async_copy(kind, kinds, kind_sem)
    fetch_kind.start()
    for n in range(count // block):
        for copy in fetch(n):
            copy.start()
    fetch_kind.wait()

    def ends(a, b, x):
        both = jnp.where(middle, 0.0, jnp.where(stop, b, a).astype(jnp.float32))
        return pltpu.roll(both, (x * 4 + 2) % TILE, 1)

    def gather(n, carry):
        for copy in fetch(n):
            copy.wait()

        def gathered(read):
            total = ends(*read(0), 0)
            for x in range(1, width):
                total = total + ends(*read(x), x)
            return total

        def cells(x):
            return pl.ds(n * block + x, rows, stride=width)

        f = [
            gathered(lambda x: (before[0, i, cells(x)], before[tiles - 1, i, cells(x)]))
            for i in range(NP)
        ]
        filled = gathered(lambda x: (solid[0, cells(x)], solid[tiles - 1, cells(x)]))
        part = pl.ds(n * rows, rows)
        k = kinds[part, pl.ds(0, TILE)], kinds[part, pl.ds((tiles - 1) * TILE, TILE)]
        idle = (filled > 0.5) | (lanes >= 4 * width)
        out = [jnp.where(idle, 0.0, v) for v in collided(f, filled > 0.5)]
        out += [filled, gathered(lambda x: k)]
        for group in range(GROUPS):
            v = out[group * GROUP]
            for m in range(1, GROUP):
                v = v + pltpu.roll(out[group * GROUP + m], m * PITCH, 1)
            packed[group, part] = v
        return carry

    lax.fori_loop(0, count // block, gather, 0)
    for face, near, moving in ((west, 0, MINUS), (east, width - 1, PLUS)):
        collide_slab(near, before, solid, post)
        for t in range(tiles):
            span = pl.ds(t * TILE, TILE)
            for n, i in enumerate(moving):
                face[n * tiles + t] = clean(post[near, i, :, span])
            here = solid[t, pl.ds(near, count // width, stride=width)]
            face[NMOVE * tiles + t] = jnp.where(here > 0, 1.0, 0.0)


def column_call(fluid, heat, mask, kind):
    depth, width, length = mask.shape
    cells = depth * width
    tiles = length // TILE
    f32 = jnp.float32
    vmem = pl.BlockSpec(memory_space=pltpu.VMEM)
    hbm = pl.BlockSpec(memory_space=pl.ANY)
    sources = (
        fluid.reshape(NF, cells, length),
        heat.reshape(NH, cells, length),
        mask.reshape(cells, length),
        kind,
    )
    return pl.pallas_call(
        functools.partial(column_kernel, width),
        in_specs=[hbm] * 4,
        out_specs=[vmem] * 6,
        out_shape=[
            jax.ShapeDtypeStruct((GROUPS, depth, TILE), f32),
            jax.ShapeDtypeStruct((tiles, NP, cells, TILE), f32),
            jax.ShapeDtypeStruct((tiles, cells, TILE), jnp.int32),
            jax.ShapeDtypeStruct((width, NP, depth, length), f32),
            jax.ShapeDtypeStruct((NFACE * tiles, depth, TILE), f32),
            jax.ShapeDtypeStruct((NFACE * tiles, depth, TILE), f32),
        ],
        scratch_shapes=[
            pltpu.VMEM((depth, length), jnp.int32),
            pltpu.SemaphoreType.DMA((depth // 8, tiles, 3)),
            pltpu.SemaphoreType.DMA,
        ],
        cost_estimate=cost(depth * width * length, 2),
        compiler_params=pltpu.CompilerParams(vmem_limit_bytes=16 * 2**20),
        name="columns",
    )(*[in_hbm(v) for v in sources])


def in_hbm(v):
    return pltpu.with_memory_space_constraint(v, pltpu.HBM)


def cost(cells, passes):
    return pl.CostEstimate(
        flops=300 * cells * passes, bytes_accessed=4 * NP * cells * passes, transcendentals=0
    )


class Lanes:
    def __init__(self, depth):
        ew, ns = lax.axis_index("ew"), lax.axis_index("ns")
        shape = (depth, TILE)
        lane = lax.broadcasted_iota(jnp.int32, shape, 1)
        level = lax.broadcasted_iota(jnp.int32, shape, 0)
        self.side, self.slot, self.j = lane // 64, (lane % 64) // 4, lane % 4
        self.ground, self.top = level == 0, level == depth - 1
        self.first, self.last = lane == 0, lane == TILE - 1
        self.west, self.east = ew == 0, ew == lax.axis_size("ew") - 1
        low = (ns == 0) & (self.side == 0) & (self.j < 2)
        high = (ns == lax.axis_size("ns") - 1) & (self.side == 1) & (self.j >= 2)
        self.beyond_y = low | high


def strip_kernel(width, own, even, odd, after, strip, to_west, to_east):
    depth = own.shape[1]
    at = Lanes(depth)
    flip = lax.axis_index("ns") % 2 == 1
    slots_w = [None] * NFACE
    slots_e = [None] * NFACE
    near_j = at.j < 2
    for group in range(GROUPS):
        o = own[group]
        above = jnp.where(flip, odd[group], even[group])
        below = jnp.where(flip, even[group], odd[group])
        low, high = jnp.where(near_j, below, o), jnp.where(near_j, o, above)
        for k in range(GROUP):
            p = group * GROUP + k
            v = jnp.where(
                at.side == 0,
                pltpu.roll(low, (16 - k * PITCH) % TILE, 1),
                pltpu.roll(high, (80 - k * PITCH) % TILE, 1),
            )
            strip[p] = v
            if p in MINUS or p == MASK:
                n = NMOVE if p == MASK else MINUS.index(p)
                slots_w[n] = pltpu.roll(v, (4 * n - 16) % TILE, 1)
            if p in PLUS or p == MASK:
                n = NMOVE if p == MASK else PLUS.index(p)
                slots_e[n] = pltpu.roll(v, (4 * n - 12 - 4 * width) % TILE, 1)
    for out, slots in ((to_west, slots_w), (to_east, slots_e)):
        total = jnp.zeros_like(slots[0])
        for n, v in enumerate(slots):
            total = jnp.where(at.slot == n, v, total)
        out[...] = total
    solid = strip[MASK] > 0.5
    for i in range(NP):
        strip[i] = jnp.where(at.beyond_y, WEIGHTS[i], jnp.where(solid, MARK, strip[i]))


def strip_call(width, own, even, odd, after):
    _, depth, _ = own.shape
    f32 = jnp.float32
    vmem = pl.BlockSpec(memory_space=pltpu.VMEM)
    return pl.pallas_call(
        functools.partial(strip_kernel, width),
        in_specs=[vmem] * 3 + [pl.BlockSpec(memory_space=pl.ANY)],
        out_specs=[vmem, vmem, vmem],
        out_shape=[
            jax.ShapeDtypeStruct((SLOTS, depth, TILE), f32),
            jax.ShapeDtypeStruct((depth, TILE), f32),
            jax.ShapeDtypeStruct((depth, TILE), f32),
        ],
        compiler_params=pltpu.CompilerParams(vmem_limit_bytes=8 * 2**20),
        name="strips",
    )(own, even, odd, after)


def raised(v, i, at):
    depth = v.shape[0]
    cz = DIRS[i][2]
    if cz == 1:
        return jnp.where(at.ground, MARK, pltpu.roll(v, 1, 0))
    if cz == -1:
        return jnp.where(at.top, WEIGHTS[i], pltpu.roll(v, depth - 1, 0))
    return v


def pieces(ref, index, i, tiles):
    return [ref[index, i, :, pl.ds(t * TILE, TILE)] for t in range(tiles)]


def turned(v, shift):
    shift = shift % TILE if isinstance(shift, int) else lax.rem(shift + 4 * TILE, TILE)
    return pltpu.roll(v, shift, 1)


def pulled(cells, cols, x, i, at):
    cx, cy, _ = DIRS[i]
    source = cells(x - cx, i)
    if cy:
        moved = [turned(v, cy) for v in source]
        lane = (x - cx + 4) * 4
        if cy == 1:
            before = [turned(cols[i], -1 - lane)] + moved[:-1]
            source = [jnp.where(at.first, p, v) for p, v in zip(before, moved)]
        else:
            after = moved[1:] + [turned(cols[i], TILE - 1 - (64 + lane + 2))]
            source = [jnp.where(at.last, n, v) for n, v in zip(after, moved)]
    return [raised(v, i, at) for v in source]


def close_strip(strip, kinds, from_west, from_east, solid, at, width):
    kind = jnp.where(at.beyond_y, 0.0, kinds)
    for face, edge, slot, moving in (
        (from_west, at.west, 3, PLUS),
        (from_east, at.east, 4 + width, MINUS),
    ):
        here = at.slot == slot
        for n, i in enumerate(moving):
            v = pltpu.roll(face, (4 * slot - 4 * n) % TILE, 1)
            v = jnp.where(solid, MARK, v)
            v = jnp.where(at.beyond_y, WEIGHTS[i], v)
            v = jnp.where(edge, ghost(i, kind) if slot == 3 else WEIGHTS[i], v)
            strip[i] = jnp.where(here, v, strip[i])


def layers(ref, tiles, halo=None):
    def cells(x, i):
        if halo is not None and isinstance(x, int) and not 0 <= x < ref.shape[0]:
            return pieces(halo, 0 if x < 0 else 1, i, tiles)
        return pieces(ref, x, i, tiles)

    return cells


def advance_slab(cells, x, strip, fresh, out, at):
    depth, length = fresh.shape[1], fresh.shape[2]
    tiles = length // TILE
    for i in range(NP):
        vs = pulled(cells, strip, x, i, at)
        for t, (v, back) in enumerate(zip(vs, cells(x, OPP[i]))):
            fresh[i, :, pl.ds(t * TILE, TILE)] = jnp.where(marked(v), back, v)
    own = cells(x, 0)
    for z in range(0, depth, 8):
        for t in range(tiles):
            part, span = pl.ds(z, 8), pl.ds(t * TILE, TILE)
            f = [fresh[i, part, span] for i in range(NP)]
            solid = marked(own[t][z : z + 8])
            for i, v in enumerate(collided(f, solid)):
                out[x, i, part, span] = v


def advance_inner_kernel(low, high, post, strip, *refs):
    out, fresh = refs[-2:]
    depth, length = post.shape[2], post.shape[3]
    at = Lanes(depth)
    cells = layers(post, length // TILE)

    def advance(x, carry):
        advance_slab(cells, x, strip, fresh, out, at)
        return carry

    lax.fori_loop(low, high, advance, 0)


def advance_inner_call(post, strip, low, high, *others):
    width, _, depth, length = post.shape
    f32 = jnp.float32
    vmem = pl.BlockSpec(memory_space=pltpu.VMEM)
    return pl.pallas_call(
        functools.partial(advance_inner_kernel, low, high),
        in_specs=[vmem] * (2 + len(others)),
        out_specs=vmem,
        out_shape=jax.ShapeDtypeStruct((width, NP, depth, length), f32),
        scratch_shapes=[pltpu.VMEM((NP, depth, length), f32)],
        input_output_aliases={2: 0} if others else {},
        cost_estimate=cost(depth * (high - low) * length, 4),
        compiler_params=pltpu.CompilerParams(vmem_limit_bytes=16 * 2**20),
        name="advance_inner",
    )(post, strip, *others)


def advance_kernel(
    post,
    west,
    east,
    strip_in,
    strip_w,
    strip_e,
    kind,
    next_in,
    next_out,
    strip2,
    to_west,
    to_east,
    halo,
    a,
    strip,
    fresh,
):
    width, depth, length = post.shape[0], post.shape[2], post.shape[3]
    tiles = length // TILE
    at = Lanes(depth)
    for p in range(SLOTS):
        strip[p] = strip_in[p]
    ends_w, ends_e = strip_w[...], strip_e[...]
    ends = jnp.where(
        at.slot == 3,
        pltpu.roll(ends_w, (12 - 4 * NMOVE) % TILE, 1),
        pltpu.roll(ends_e, (16 + 4 * width - 4 * NMOVE) % TILE, 1),
    )
    kind_end = pltpu.roll(strip[KIND], TILE - 4, 1)
    close_strip(strip, kind_end, ends_w, ends_e, ends > 0.5, at, width)
    halo[0], halo[1] = ends, kind_end
    for n, face in ((2, west), (2 + tiles, east)):
        for t in range(tiles):
            halo[n + t] = face[NMOVE * tiles + t]
    kinds = kind[...].astype(jnp.float32)
    close_faces(a, west, east, halo, kinds, at)

    for i in range(NP):
        cx, cy, _ = DIRS[i]
        v = strip[i]
        if cx or cy:
            v = pltpu.roll(v, (4 * cx + cy) % TILE, 1)
        v = raised(v, i, at)
        fresh[i, :, pl.ds(0, TILE)] = jnp.where(marked(v), strip[OPP[i]], v)
    for z in range(0, depth, 8):
        part = pl.ds(z, 8)
        f = [fresh[i, part, pl.ds(0, TILE)] for i in range(NP)]
        outside = at.beyond_y[z : z + 8]
        for i, v in enumerate(collided(f, marked(strip[0, part]))):
            strip2[i, part] = jnp.where(outside, WEIGHTS[i], v)

    cells = layers(post, tiles, a)
    for x in (0, width - 1):
        advance_slab(cells, x, strip, fresh, next_out, at)
    for out, near, moving in ((to_west, 0, MINUS), (to_east, width - 1, PLUS)):
        slots = None
        for n, i in enumerate(moving):
            for t in range(tiles):
                out[n * tiles + t] = clean(next_out[near, i, :, pl.ds(t * TILE, TILE)])
            v = pltpu.roll(clean(strip2[i]), (4 * n - 4 * (near + 4)) % TILE, 1)
            slots = v if slots is None else jnp.where(at.slot == n, v, slots)
        out[NMOVE * tiles] = slots


def advance_call(post, west, east, strip, strip_w, strip_e, kind, inner):
    width, _, depth, length = post.shape
    tiles = length // TILE
    f32 = jnp.float32
    vmem = pl.BlockSpec(memory_space=pltpu.VMEM)
    sends = NMOVE * tiles + 1
    return pl.pallas_call(
        advance_kernel,
        in_specs=[vmem] * 8,
        out_specs=[vmem] * 5,
        out_shape=[
            jax.ShapeDtypeStruct((width, NP, depth, length), f32),
            jax.ShapeDtypeStruct((NP, depth, TILE), f32),
            jax.ShapeDtypeStruct((sends, depth, TILE), f32),
            jax.ShapeDtypeStruct((sends, depth, TILE), f32),
            jax.ShapeDtypeStruct((2 + 2 * tiles, depth, TILE), f32),
        ],
        scratch_shapes=[
            pltpu.VMEM((2, NP, depth, length), f32),
            pltpu.VMEM((SLOTS, depth, TILE), f32),
            pltpu.VMEM((NP, depth, length), f32),
        ],
        input_output_aliases={7: 0},
        cost_estimate=cost(depth * 2 * length, 3),
        compiler_params=pltpu.CompilerParams(vmem_limit_bytes=24 * 2**20),
        name="advance",
    )(post, west, east, strip, strip_w, strip_e, kind, inner)


def close_faces(a, west, east, halo, kinds, at):
    tiles = a.shape[3] // TILE
    for face, edge, near, moving in (
        (west, at.west, 0, PLUS),
        (east, at.east, 1, MINUS),
    ):
        for t in range(tiles):
            solid = halo[2 + t if near == 0 else 2 + tiles + t] > 0.5
            span = slice(t * TILE, (t + 1) * TILE)
            for n, i in enumerate(moving):
                v = jnp.where(solid, MARK, face[n * tiles + t])
                outer = ghost(i, kinds[:, span]) if near == 0 else WEIGHTS[i]
                a[near, i, :, span] = jnp.where(edge, outer, v)


def settle_slab(cells, x, strip, before, out, at):
    _, _, count, _ = before.shape
    depth = out.shape[1]
    own = pl.ds(x, depth, stride=count // depth)
    solids = [marked(v) for v in cells(x, 0)]
    for i in range(NP):
        vs = pulled(cells, strip, x, i, at)
        for t, (v, back) in enumerate(zip(vs, cells(x, OPP[i]))):
            span = pl.ds(t * TILE, TILE)
            v = jnp.where(marked(v), back, v)
            out[i, :, span] = jnp.where(solids[t], before[t, i, own], v)


def stores(buffer, fluid_out, heat_out, x, sem):
    return (
        pltpu.make_async_copy(buffer.at[pl.ds(0, NF)], fluid_out.at[:, :, x], sem.at[0]),
        pltpu.make_async_copy(buffer.at[pl.ds(NF, NH)], heat_out.at[:, :, x], sem.at[1]),
    )


def settle_inner_kernel(before, post, strip, fluid_out, heat_out, buffer, sem):
    width, depth, length = post.shape[0], post.shape[2], post.shape[3]
    at = Lanes(depth)
    cells = layers(post, length // TILE)

    def settle(x, carry):
        settle_slab(cells, x, strip, before, buffer.at[x], at)
        for copy in stores(buffer.at[x], fluid_out, heat_out, x, sem.at[x]):
            copy.start()
        return carry

    lax.fori_loop(1, width - 1, settle, 0)
    for x in range(1, width - 1):
        for copy in stores(buffer.at[x], fluid_out, heat_out, x, sem.at[x]):
            copy.wait()


def settle_inner_call(before, post, strip, outs):
    width, _, depth, length = post.shape
    vmem = pl.BlockSpec(memory_space=pltpu.VMEM)
    hbm = pl.BlockSpec(memory_space=pl.ANY)
    return pl.pallas_call(
        settle_inner_kernel,
        in_specs=[vmem] * 3,
        out_specs=[hbm, hbm],
        out_shape=[jax.ShapeDtypeStruct(v.shape, v.dtype) for v in outs],
        scratch_shapes=[
            pltpu.VMEM((width, NP, depth, length), jnp.float32),
            pltpu.SemaphoreType.DMA((width, 2)),
        ],
        cost_estimate=cost(depth * width * length, 3),
        compiler_params=pltpu.CompilerParams(vmem_limit_bytes=24 * 2**20),
        name="settle_inner",
    )(before, post, strip)


def settle_kernel(
    before,
    post,
    west,
    east,
    strip_in,
    halo,
    kind,
    fluid_in,
    heat_in,
    fluid_out,
    heat_out,
    b,
    strip,
    buffer,
    sem,
):
    width, depth, length = post.shape[0], post.shape[2], post.shape[3]
    tiles = length // TILE
    at = Lanes(depth)
    for p in range(NP):
        strip[p] = strip_in[p]
    ends_w, ends_e = west[NMOVE * tiles], east[NMOVE * tiles]
    close_strip(strip, halo[1], ends_w, ends_e, halo[0] > 0.5, at, width)
    close_faces(b, west, east, halo, kind[...].astype(jnp.float32), at)
    cells = layers(post, tiles, b)
    ends = ((0, 0), (1, width - 1))
    for n, x in ends:
        settle_slab(cells, x, strip, before, buffer.at[n], at)
        for copy in stores(buffer.at[n], fluid_out, heat_out, x, sem.at[n]):
            copy.start()
    for n, x in ends:
        for copy in stores(buffer.at[n], fluid_out, heat_out, x, sem.at[n]):
            copy.wait()


def settle_call(before, post, west, east, strip, halo, kind, inner):
    _, _, depth, length = post.shape
    f32 = jnp.float32
    vmem = pl.BlockSpec(memory_space=pltpu.VMEM)
    hbm = pl.BlockSpec(memory_space=pl.ANY)
    return pl.pallas_call(
        settle_kernel,
        in_specs=[vmem] * 7 + [hbm] * 2,
        out_specs=[hbm, hbm],
        out_shape=[jax.ShapeDtypeStruct(v.shape, v.dtype) for v in inner],
        scratch_shapes=[
            pltpu.VMEM((2, NP, depth, length), f32),
            pltpu.VMEM((NP, depth, TILE), f32),
            pltpu.VMEM((2, NP, depth, length), f32),
            pltpu.SemaphoreType.DMA((2, 2)),
        ],
        input_output_aliases={7: 0, 8: 1},
        cost_estimate=cost(depth * 2 * length, 3),
        compiler_params=pltpu.CompilerParams(vmem_limit_bytes=24 * 2**20),
        name="settle",
    )(before, post, west, east, strip, halo, kind, *inner)


def ring(v, axis, shift):
    n = lax.axis_size(axis)
    return lax.ppermute(v, axis, [(i, (i + shift) % n) for i in range(n)])


def swap(v, axis, odd):
    n = lax.axis_size(axis)
    pairs = [(i, i + 1) for i in range(odd, n - 1, 2)]
    return lax.ppermute(v, axis, pairs + [(j, i) for i, j in pairs])


def per_device(fluid, heat, solid_mask, inflow_type):
    width = solid_mask.shape[1]
    own, before, solid, ends, to_west, to_east = column_call(
        fluid, heat, solid_mask, inflow_type
    )
    even = swap(own, "ns", 0)
    odd = swap(own, "ns", 1)
    west = ring(to_east, "ew", 1)
    east = ring(to_west, "ew", -1)
    post = collide_call(before, solid, ends)
    strip, to_west, to_east = strip_call(width, own, even, odd, post)
    strip_w, strip_e = ring(to_east, "ew", 1), ring(to_west, "ew", -1)
    middle = 1 + MIDDLE
    done = advance_inner_call(post, strip, 1, middle)
    done, strip2, to_west, to_east, halo = advance_call(
        post, west, east, strip, strip_w, strip_e, inflow_type, done
    )
    west, east = ring(to_east, "ew", 1), ring(to_west, "ew", -1)
    post = advance_inner_call(post, strip, middle, width - 1, done)
    inner = settle_inner_call(before, post, strip2, (fluid, heat))
    return settle_call(before, post, west, east, strip2, halo, inflow_type, inner)


def solution(mesh):
    return jax.shard_map(
        per_device,
        mesh=mesh,
        in_specs=(
            P(None, None, "ew", "ns"),
            P(None, None, "ew", "ns"),
            P(None, "ew", "ns"),
            P(None, "ns"),
        ),
        out_specs=(P(None, None, "ew", "ns"), P(None, None, "ew", "ns")),
        check_vma=False,
    )
```
